512 devices in a mesh: row: 64 (over y, z), col: 8 (over x, core).
Axes of the slice: x: 4, y: 4, z: 16, core: 2. Of those that a mesh axis runs over, the one named last changes fastest.
Arguments:
- sketch: bfloat16 [65536, 128], P(('row', 'col')), may hold values from -6 to 6
- degree: float32 [65536], P(('row', 'col')), may hold values from 1 to 64
- block_vals: bfloat16 [64, 8, 16, 128, 128], P('row', 'col'), may hold values from -0.125 to 0.125
- block_rows: int32 [64, 8, 16], P('row', 'col'), may hold values from 0 to 7
- block_cols: int32 [64, 8, 16], P('row', 'col'), may hold values from 0 to 63
- live_count: int32 [64, 8], P('row', 'col'), may hold values from 2 to 16, as said below
Outputs:
- basis: float32 [65536, 128], P(('row', 'col'))
- factor: float32 [128, 128], replicated
The draws below stay inside these ranges and needn't reach their ends.
Inputs may be any that keep to these rules, and one draw needn't show every extreme that they name: Slots at or past live_count of a device are ignored; some device has all 16 slots live.
All inputs are finite; a program needn't handle non-finite values.
Results may differ from the reference program's by a relative error of at most 0.003.
Values may be sent and summed in bfloat16 or wider, within the bound.
A program may use at most 64 MiB of HBM per device.

```python
import math
import jax
import jax.numpy as jnp
from jax import lax

RANK = 128
BLK = 128
ROWS_DEV = 128
NNZ_DEV = 16
ITERS = 1
BLK_DEV = 1
ROW_GROUPS = 64
COL_GROUPS = 8
ROW_BLOCKS = 8
COL_BLOCKS = 64
NODES = 65536


def draw_live_count(key, part):
    first = jax.random.fold_in(key, 71)
    second = jax.random.fold_in(key, 72)
    third = jax.random.fold_in(key, 73)
    total = ROW_GROUPS * COL_GROUPS
    counts = jax.random.randint(first, (total,), NNZ_DEV // 8, NNZ_DEV // 2 + 1)
    heavy = jax.random.randint(second, (total,), 0, 10) == 0
    counts = jnp.where(heavy, NNZ_DEV, counts)
    chosen = jax.random.randint(third, (), 0, total)
    counts = counts.at[chosen].set(NNZ_DEV)
    return counts.astype(jnp.int32).reshape(ROW_GROUPS, COL_GROUPS)


def with_ends(result, own_key, smallest, top_value):
    longest = result.shape.index(max(result.shape))
    spots = []
    for shift in (0, 1):
        where = [jax.random.randint(jax.random.fold_in(own_key, axis), (), 0, length) for axis, length in enumerate(result.shape)]
        where[longest] = (where[longest] + shift) % result.shape[longest]
        spots.append(tuple(where))
    return result.at[spots[0]].set(smallest).at[spots[1]].set(top_value)


def steps_of(key, shape, split, smallest, largest):
    gain = 1.0
    for axis_at, blocks in split:
        heights = jax.random.uniform(jax.random.fold_in(jax.random.fold_in(key, 6), axis_at), (blocks,), jnp.float32, smallest / len(split), largest / len(split))
        gain = gain * jnp.repeat(jnp.exp(heights), shape[axis_at] // blocks).reshape((-1,) + (1,) * (len(shape) - 1 - axis_at))
    return gain


def scatter_about(key, dims, deviation, reach, split=(), held_as=jnp.bfloat16):
    drawn = jax.random.normal(key, dims, jnp.float32) * deviation
    if len(split) > 0:
        drawn = steps_of(key, dims, split, -0.22, 0.18) * drawn
    return jnp.clip(drawn, min=-reach, max=reach).astype(held_as)


def setup_inputs(seed: int = 0) -> dict:
    streams_of = jax.random.split(jax.random.key(seed), 7)
    sketch = scatter_about(streams_of[0], (NODES, RANK), 1.0, 6.0, ((0, 512),))
    degree = jnp.clip(jnp.exp(math.log(64.0) - 4.158883 * jax.random.uniform(streams_of[1], (NODES,), jnp.float32) ** steps_of(streams_of[1], (NODES,), ((0, 512),), -0.2, 0.2)), 1.0, 64.0)
    block_vals = scatter_about(streams_of[2], (ROW_GROUPS, COL_GROUPS, NNZ_DEV, BLK, BLK), (NNZ_DEV * BLK * BLK // ROWS_DEV) ** -0.5, 0.125, ((0, 64), (1, 8)))
    block_rows = with_ends(jax.random.randint(streams_of[3], (ROW_GROUPS, COL_GROUPS, NNZ_DEV), 0, ROW_BLOCKS), jax.random.fold_in(streams_of[3], 1), 0, ROW_BLOCKS - 1).astype(jnp.int32)
    block_cols = with_ends(jax.random.randint(streams_of[4], (ROW_GROUPS, COL_GROUPS, NNZ_DEV), 0, COL_BLOCKS), jax.random.fold_in(streams_of[4], 1), 0, COL_BLOCKS - 1).astype(jnp.int32)
    live_count = draw_live_count(jax.random.fold_in(streams_of[6], 71), 0)
    return dict(sketch=sketch, degree=degree, block_vals=block_vals, block_rows=block_rows, block_cols=block_cols, live_count=live_count)


def apply_blocks(moved, block_vals, block_rows, block_cols, live_count):
    rank = moved.shape[1]
    grouped = moved.reshape(ROW_GROUPS, COL_GROUPS, BLK_DEV, BLK, rank)
    columns = jnp.transpose(grouped, (1, 0, 2, 3, 4)).reshape(COL_GROUPS, COL_BLOCKS, BLK, rank)
    group_ids = jnp.arange(COL_GROUPS, dtype=jnp.int32)[:, None]
    slot_ids = jnp.arange(NNZ_DEV, dtype=jnp.int32)
    block_ids = jnp.arange(ROW_BLOCKS, dtype=jnp.int32)

    def stripe(inputs):
        values, rows_here, cols_here, live_here = inputs
        picked = columns[group_ids, cols_here].astype(jnp.float32)
        products = jnp.einsum('cnab,cnbk->cnak', values.astype(jnp.float32), picked)
        live = slot_ids[None, :] < live_here[:, None]
        table = ((rows_here[:, :, None] == block_ids[None, None, :]) & live[:, :, None]).astype(jnp.float32)
        return jnp.einsum('cnr,cnak->rak', table, products, precision=lax.Precision.HIGHEST)
    stripes = lax.map(stripe, (block_vals, block_rows, block_cols, live_count))
    return stripes.reshape(NODES, rank)

def reference(sketch, degree, block_vals, block_rows, block_cols, live_count):
    scale = lax.rsqrt(degree)
    basis = sketch.astype(jnp.float32)
    lower = jnp.zeros((RANK, RANK), jnp.float32)
    for step in range(ITERS):
        moved = (scale[:, None] * basis).astype(jnp.bfloat16)
        image = scale[:, None] * apply_blocks(moved, block_vals, block_rows, block_cols, live_count)
        gram = jnp.dot(image.T, image, precision=lax.Precision.HIGHEST) / NODES
        lower = jnp.linalg.cholesky(gram)
        basis = jax.scipy.linalg.solve_triangular(lower, image.T, lower=True).T
    return (basis, lower.T)
```

```python
import functools

import jax
import jax.numpy as jnp
from jax import lax
from jax.experimental import pallas as pl
from jax.experimental.pallas import tpu as pltpu
from jax.sharding import PartitionSpec as P

MESH = pl.DeviceIdType.MESH
HIGHEST = lax.Precision.HIGHEST
NX, NY, NZ = 4, 4, 16
BLK = 128
SLOTS = 16
ZFIRST = 128


def halves(lo, hi):
    mid = lo + (hi - lo + 31) // 32 * 16
    return {1: (lo, mid), -1: (mid, hi)}


def gather_plan():
    plan = []
    if ZFIRST > 0:
        half = halves(0, ZFIRST)
        for s in range(NZ // 2):
            for d in (1, -1):
                lo, hi = (0, ZFIRST) if s < NZ // 2 - 1 else half[d]
                plan.append((s, 0, d, 0, -d * s, lo, hi))
        for oz in range(1 - NZ // 2, NZ // 2 + 1):
            for d in (1, -1):
                plan.append((abs(oz) + 0.2, d, 0, 0, oz, 0, ZFIRST))
                lo, hi = half[d]
                plan.append((abs(oz) + 1.1, d, 0, -d, oz, lo, hi))
    if ZFIRST < BLK:
        half = halves(ZFIRST, BLK)
        for d in (1, -1):
            plan.append((0, d, 0, 0, 0, ZFIRST, BLK))
            lo, hi = half[d]
            plan.append((1, d, 0, -d, 0, lo, hi))
        for oy, start in ((0, 0), (-1, 1), (1, 1), (2, 2)):
            for s in range(NZ // 2):
                for d in (1, -1):
                    lo, hi = (ZFIRST, BLK) if s < NZ // 2 - 1 else half[d]
                    plan.append((start + s + 0.3, 0, d, oy, -d * s, lo, hi))
    return sorted(plan, key=lambda m: m[0])


def wrap(value, n):
    value = value % n
    return value - n if value > n // 2 else value


PLAN = gather_plan()
N_PLAN = len(PLAN)


def row_of(y, z):
    return lax.rem(y + 4 * NY, NY) * NZ + lax.rem(z + 4 * NZ, NZ)


def comm_kernel(sk_ref, deg_ref, vals_hbm, rows_ref, cols_ref, live_ref, gram_ref, image_ref,
                gat, vals, prods, part, crecv, comb, xrecv, glocal, rsbuf, zbuf, tile,
                vsem, gs, gr, cs, cr, xs, xr, rs_s, rs_r, z_s, z_r, ag_s, ag_r):
    row = lax.axis_index("row")
    col = lax.axis_index("col")
    y, z = row // NZ, lax.rem(row, NZ)
    x, core = col // 2, lax.rem(col, 2)

    barrier = pltpu.get_barrier_semaphore()
    peers = [(row_of(y, z + 1), col), (row_of(y, z - 1), col), (row_of(y + 1, z), col), (row_of(y - 1, z), col)]
    peers += [(row, lax.rem(col + k, 2 * NX)) for k in range(1, 2 * NX)]
    for peer in peers:
        pl.semaphore_signal(barrier, inc=1, device_id=peer, device_id_type=MESH)
    load_vals = pltpu.make_async_copy(vals_hbm, vals, vsem)
    load_vals.start()

    ids_r = lax.broadcasted_iota(jnp.int32, (BLK, BLK), 0)
    ids_c = lax.broadcasted_iota(jnp.int32, (BLK, BLK), 1)
    spread = jnp.where(ids_r == ids_c, jnp.broadcast_to(deg_ref[...], (BLK, BLK)), 0.0)
    scale = lax.rsqrt(jnp.sum(spread, axis=1, keepdims=True))
    gat[row] = (scale * sk_ref[...].astype(jnp.float32)).astype(jnp.bfloat16)
    pl.semaphore_wait(barrier, len(peers))

    def message(i):
        _, dy, dz, oy, oz, lo, hi = PLAN[i]
        block = gat.at[row_of(y + oy, z + oz), pl.ds(lo, hi - lo), :]
        return pltpu.make_async_remote_copy(
            src_ref=block, dst_ref=block, send_sem=gs.at[i], recv_sem=gr.at[i],
            device_id=(row_of(y + dy, z + dz), col), device_id_type=MESH)

    def landed(i):
        _, dy, dz, oy, oz, lo, hi = PLAN[i]
        block = gat.at[row_of(y + oy - dy, z + oz - dz), pl.ds(lo, hi - lo), :]
        pltpu.make_async_remote_copy(
            src_ref=block, dst_ref=block, send_sem=gs.at[i], recv_sem=gr.at[i],
            device_id=(row_of(y + dy, z + dz), col), device_id_type=MESH).wait_recv()

    waited = set()
    for i, (_, dy, dz, oy, oz, lo, hi) in enumerate(PLAN):
        for j, (_, ey, ez, py, pz, plo, phi) in enumerate(PLAN):
            here = (wrap(py - ey, NY), wrap(pz - ez, NZ)) == (wrap(oy, NY), wrap(oz, NZ))
            if here and plo < hi and lo < phi and j not in waited:
                landed(j)
                waited.add(j)
        message(i).start()
    for j in range(N_PLAN):
        if j not in waited:
            landed(j)

    load_vals.wait()
    for s in range(SLOTS):
        picked = gat[cols_ref[s]]
        prods[s] = jnp.dot(vals[s], picked, preferred_element_type=jnp.float32)
    live = live_ref[0]
    for r in range(2 * NX):
        weights = [jnp.where((rows_ref[s] == r) & (s < live), 1.0, 0.0) for s in range(SLOTS)]
        for k in range(BLK // 16):
            lines = pl.ds(k * 16, 16)
            total = weights[0] * prods[0, lines, :]
            for s in range(1, SLOTS):
                total = total + weights[s] * prods[s, lines, :]
            part[r % 2, r // 2, lines, :] = total

    other = 1 - core
    swap = pltpu.make_async_remote_copy(
        src_ref=part.at[other], dst_ref=crecv, send_sem=cs, recv_sem=cr,
        device_id=(row, x * 2 + other), device_id_type=MESH)
    swap.start()
    swap.wait_recv()
    sends = []
    for k in (2, 1, 3):
        to = lax.rem(x + k, NX)
        comb[k] = part[core, to] + crecv[to]
        send = pltpu.make_async_remote_copy(
            src_ref=comb.at[k], dst_ref=xrecv.at[k], send_sem=xs.at[k], recv_sem=xr.at[k],
            device_id=(row, to * 2 + core), device_id_type=MESH)
        send.start()
        sends.append(send)
    total = part[core, x] + crecv[x]
    for send in (sends[1], sends[2], sends[0]):
        send.wait_recv()
    for k in (1, 2, 3):
        total = total + xrecv[k]
    image = scale * total
    image_ref[...] = image
    glocal[...] = lax.dot_general(image, image, (((0,), (0,)), ((), ())), precision=HIGHEST,
                                  preferred_element_type=jnp.float32)

    chip = x * NY + y
    me = chip * 2 + core
    keeper = lax.rem(x + y, 2)
    owner = core == keeper

    def plane(t):
        tx, ty = t // NY, lax.rem(t, NY)
        return tx, ty, lax.rem(tx + ty, 2)

    def scatter(k):
        t = lax.rem(chip + k, NX * NY)
        tx, ty, tc = plane(t)
        return pltpu.make_async_remote_copy(
            src_ref=glocal.at[pl.ds(pl.multiple_of(t * 8, 8), 8), :], dst_ref=rsbuf.at[me],
            send_sem=rs_s.at[k], recv_sem=rs_r.at[me],
            device_id=(row_of(ty, z), tx * 2 + tc), device_id_type=MESH)

    def keep(k):
        t = lax.rem(chip + k, NX * NY)
        tx, ty, _ = plane(t)
        return tx, ty, t

    for k in list(range(1, NX * NY)):
        scatter(k).start()

    @pl.when(jnp.logical_not(owner))
    def _():
        scatter(0).start()

    mine = pl.ds(pl.multiple_of(chip * 8, 8), 8)

    @pl.when(owner)
    def _():
        total = glocal[mine, :]
        for k in range(1, 2 * NX * NY):
            src = lax.rem(me + k, 2 * NX * NY)
            pltpu.make_async_remote_copy(
                src_ref=rsbuf.at[src], dst_ref=rsbuf.at[src], send_sem=rs_s.at[0], recv_sem=rs_r.at[src],
                device_id=(row, x * 2 + other), device_id_type=MESH).wait_recv()
        for k in range(1, 2 * NX * NY):
            total = total + rsbuf[lax.rem(me + k, 2 * NX * NY)]
        zbuf[z] = total

        def along(k):
            return pltpu.make_async_remote_copy(
                src_ref=zbuf.at[z], dst_ref=zbuf.at[z], send_sem=z_s.at[k], recv_sem=z_r.at[z],
                device_id=(row_of(y, z + k), col), device_id_type=MESH)

        order = sorted(range(1, NZ), key=lambda k: -min(k, NZ - k))
        for k in order:
            along(k).start()
        for k in reversed(order):
            src = lax.rem(z + k, NZ)
            pltpu.make_async_remote_copy(
                src_ref=zbuf.at[src], dst_ref=zbuf.at[src], send_sem=z_s.at[k], recv_sem=z_r.at[src],
                device_id=(row_of(y, z + k), col), device_id_type=MESH).wait_recv()
        total = zbuf[0]
        for k in range(1, NZ):
            total = total + zbuf[k]
        gram_ref[mine, :] = total

        def back(k):
            if k == 0:
                device = (row, x * 2 + other)
            else:
                t = lax.rem(chip + k // 2, NX * NY)
                device = (row_of(lax.rem(t, NY), z), t // NY * 2 + k % 2)
            return pltpu.make_async_remote_copy(
                src_ref=gram_ref.at[mine, :], dst_ref=gram_ref.at[mine, :], send_sem=ag_s.at[k],
                recv_sem=ag_r.at[chip], device_id=device, device_id_type=MESH)

        spots = [0] + list(range(2, 2 * NX * NY))
        for k in spots[::-1]:
            back(k).start()
        for k in order:
            along(k).wait_send()
        for k in spots:
            back(k).wait_send()

    def arrive(t):
        lines = pl.ds(pl.multiple_of(t * 8, 8), 8)
        pltpu.make_async_remote_copy(
            src_ref=gram_ref.at[lines, :], dst_ref=gram_ref.at[lines, :], send_sem=ag_s.at[0],
            recv_sem=ag_r.at[t], device_id=(row, x * 2 + other), device_id_type=MESH).wait_recv()

    for k in range(1, NX * NY):
        arrive(lax.rem(chip + k, NX * NY))

    @pl.when(jnp.logical_not(owner))
    def _():
        arrive(chip)
        scatter(0).wait_send()

    for i in range(N_PLAN):
        message(i).wait_send()
    swap.wait_send()
    for send in sends:
        send.wait_send()
    for k in range(1, NX * NY):
        scatter(k).wait_send()


def factor_kernel(nodes, gram_ref, image_ref, basis_ref, factor_ref, inv_ref):
    tiles = BLK // 8
    left = [gram_ref[pl.ds(k * 8, 8), :] * (1.0 / nodes) for k in range(tiles)]
    row_ids = lax.broadcasted_iota(jnp.int32, (8, BLK), 0)
    lane_ids = lax.broadcasted_iota(jnp.int32, (8, BLK), 1)
    right = [jnp.where(row_ids + 8 * k == lane_ids, 1.0, 0.0) for k in range(tiles)]
    for j in range(BLK):
        k0, r = divmod(j, 8)
        pivot = left[k0][r:r + 1, j:j + 1]
        inv = lax.rsqrt(pivot)
        up_left = left[k0][r:r + 1, :] * inv
        up_right = right[k0][r:r + 1, :] * inv
        factor_ref[pl.ds(j, 1), :] = jnp.where(lane_ids[:1] >= j, up_left, 0.0)
        inv_ref[pl.ds(j, 1), :] = up_right
        for k in range(k0, tiles):
            by = left[k][:, j:j + 1] * inv
            if k == k0:
                if r == 7:
                    continue
                by = jnp.where(row_ids[:, :1] > r, by, 0.0)
            left[k] = left[k] - by * up_left
            right[k] = right[k] - by * up_right
    basis_ref[...] = lax.dot_general(image_ref[...], inv_ref[...], (((1,), (1,)), ((), ())), precision=HIGHEST,
                                     preferred_element_type=jnp.float32)


def local(sketch, degree, block_vals, block_rows, block_cols, live_count):
    f32 = jnp.float32
    square = jax.ShapeDtypeStruct((BLK, BLK), f32)
    vmem = pl.BlockSpec(memory_space=pltpu.VMEM)
    smem = pl.BlockSpec(memory_space=pltpu.SMEM)
    dma = pltpu.SemaphoreType.DMA
    gram, image = pl.pallas_call(
        comm_kernel,
        out_shape=(square, square),
        in_specs=[vmem, vmem, pl.BlockSpec(memory_space=pl.ANY), smem, smem, smem],
        out_specs=(vmem, vmem),
        scratch_shapes=[
            pltpu.VMEM((NY * NZ, BLK, BLK), jnp.bfloat16),
            pltpu.VMEM((SLOTS, BLK, BLK), jnp.bfloat16),
            pltpu.VMEM((SLOTS, BLK, BLK), f32),
            pltpu.VMEM((2, NX, BLK, BLK), f32),
            pltpu.VMEM((NX, BLK, BLK), f32),
            pltpu.VMEM((NX, BLK, BLK), f32),
            pltpu.VMEM((NX, BLK, BLK), f32),
            pltpu.VMEM((BLK, BLK), f32),
            pltpu.VMEM((2 * NX * NY, 8, BLK), f32),
            pltpu.VMEM((NZ, 8, BLK), f32),
            pltpu.VMEM((8, BLK), f32),
            dma, dma((N_PLAN,)), dma((N_PLAN,)), dma, dma, dma((NX,)), dma((NX,)),
            dma((NX * NY,)), dma((2 * NX * NY,)), dma((NZ,)), dma((NZ,)), dma((2 * NX * NY,)), dma((NX * NY,)),
        ],
        compiler_params=pltpu.CompilerParams(collective_id=0, has_side_effects=True),
        name="spread",
    )(sketch, degree.reshape(1, BLK), block_vals.reshape(SLOTS, BLK, BLK), block_rows.reshape(SLOTS),
      block_cols.reshape(SLOTS), live_count.reshape(1))
    nodes = BLK * lax.axis_size("row") * lax.axis_size("col")
    return pl.pallas_call(
        functools.partial(factor_kernel, nodes),
        out_shape=(square, square),
        in_specs=[vmem, vmem],
        out_specs=(vmem, vmem),
        scratch_shapes=[pltpu.VMEM((BLK, BLK), f32)],
        name="orthonormalize",
    )(gram, image)


def solution(mesh):
    in_specs = (
        P(("row", "col"), None),
        P(("row", "col")),
        P("row", "col", None, None, None),
        P("row", "col", None),
        P("row", "col", None),
        P("row", "col"),
    )
    out_specs = (P(("row", "col"), None), P())
    return jax.shard_map(local, mesh=mesh, in_specs=in_specs, out_specs=out_specs, check_vma=False)
```

```python
import functools

import jax
import jax.numpy as jnp
from jax import lax
from jax.experimental import pallas as pl
from jax.experimental.pallas import tpu as pltpu
from jax.sharding import PartitionSpec as P

MESH = pl.DeviceIdType.MESH
HIGHEST = lax.Precision.HIGHEST
NX, NY, NZ = 4, 4, 16
BLK = 128
SLOTS = 16

PLAN = (
    (1, 0, 0, 0, 1, 96, 128),
    (-1, 0, 0, 0, 1, 96, 128),
    (0, 3, 0, 0, 1, 0, 96),
    (0, -3, 0, 0, 1, 0, 96),
    (0, 1, 0, 0, 1, 0, 96),
    (0, -1, 0, 0, 1, 0, 96),
    (1, 0, 0, 0, 1, 0, 96),
    (-1, 0, 0, 0, 1, 0, 96),
    (1, 0, -1, 0, 1, 96, 112),
    (-1, 0, 1, 0, 1, 112, 128),
    (1, 0, -1, 0, 1, 0, 48),
    (-1, 0, 1, 0, 1, 48, 96),
    (0, 3, 0, -3, 1, 0, 96),
    (0, -3, 0, 3, 1, 0, 96),
    (0, -1, 0, -3, 1, 0, 96),
    (0, 1, 0, -3, 1, 0, 96),
    (0, 3, None, 0, 1, 96, 128),
    (0, -3, None, 0, 1, 96, 128),
    (0, 1, 0, 3, 1, 0, 96),
    (0, -1, 0, 3, 1, 0, 96),
    (1, 0, 0, 1, 1, 0, 96),
    (-1, 0, 0, 1, 1, 0, 96),
    (1, 0, 0, -1, 1, 0, 96),
    (-1, 0, 0, -1, 1, 0, 96),
    (0, 1, None, 0, 1, 96, 128),
    (0, -1, None, 0, 1, 96, 128),
    (0, 1, 0, -6, 1, 0, 96),
    (0, -1, 0, 6, 1, 0, 96),
    (0, -1, 0, -6, 1, 0, 96),
    (0, 1, 0, 6, 1, 0, 96),
    (1, 0, 0, -3, 2, 0, 96),
    (-1, 0, 0, -3, 2, 0, 96),
    (1, 0, -1, 1, 1, 0, 48),
    (-1, 0, 1, 1, 1, 48, 96),
    (1, 0, -1, -1, 1, 0, 48),
    (-1, 0, 1, -1, 1, 48, 96),
    (0, 3, None, -3, 1, 96, 128),
    (0, -3, None, 3, 1, 96, 128),
    (0, -1, None, -3, 1, 96, 128),
    (0, 1, None, -3, 1, 96, 128),
    (0, 1, None, 3, 1, 96, 128),
    (1, 0, 0, 2, 2, 0, 96),
    (-1, 0, 0, 2, 2, 0, 96),
    (0, -1, None, 3, 1, 96, 128),
    (1, 0, -1, -3, 2, 0, 48),
    (-1, 0, 1, -3, 2, 48, 96),
    (0, 1, 0, -7, 1, 0, 48),
    (0, -1, 0, 7, 1, 48, 96),
    (1, 0, 0, 6, 2, 0, 96),
    (-1, 0, 0, 6, 2, 0, 96),
    (1, 0, 0, 4, 2, 0, 96),
    (-1, 0, 0, 4, 2, 0, 96),
    (1, 0, 0, -5, 2, 0, 96),
    (-1, 0, 0, -5, 2, 0, 96),
    (1, 0, 0, -7, 2, 0, 96),
    (-1, 0, 0, -7, 2, 0, 96),
    (1, 0, -1, 2, 2, 0, 48),
    (-1, 0, 1, 2, 2, 48, 96),
    (0, 1, None, -6, 1, 96, 128),
    (0, -1, None, 6, 1, 96, 128),
    (0, -1, None, -6, 1, 96, 128),
    (0, 1, None, 6, 1, 96, 128),
    (1, 0, -1, 6, 2, 0, 48),
    (-1, 0, 1, 6, 2, 48, 96),
    (1, 0, 0, 8, 1, 0, 96),
    (-1, 0, 0, 8, 1, 0, 96),
    (1, 0, -1, 4, 2, 0, 48),
    (-1, 0, 1, 4, 2, 48, 96),
    (0, 1, None, -7, 1, 96, 112),
    (0, -1, None, 7, 1, 112, 128),
    (1, 0, -1, -5, 2, 0, 48),
    (-1, 0, 1, -5, 2, 48, 96),
    (1, 0, -1, -7, 2, 0, 48),
    (-1, 0, 1, -7, 2, 48, 96),
    (1, 0, -1, 8, 1, 0, 48),
    (-1, 0, 1, 8, 1, 48, 96),
)
N_PLAN = len(PLAN)
LOW = NZ // 2 - 1


def wrap(value, n):
    value = value % n
    return value - n if value > n // 2 else value


def row_of(y, z):
    return lax.rem(y + 4 * NY, NY) * NZ + lax.rem(z + 4 * NZ, NZ)


def comm_kernel(sk_any, deg_any, vals_any, rows_any, cols_any, live_any, gram_ref, image_ref,
                sk_ref, deg_ref, rows_ref, cols_ref, live_ref, gat, vals, prods, part, crecv, comb, xrecv, glocal, rsbuf, zbuf,
                vsem, gs, gr, cs, cr, xs, xr, rs_s, rs_r, z_s, z_r, ag_s, ag_r):
    row = lax.axis_index("row")
    col = lax.axis_index("col")
    y, z = row // NZ, lax.rem(row, NZ)
    x, core = col // 2, lax.rem(col, 2)

    loads = [pltpu.make_async_copy(src, dst, vsem.at[i]) for i, (src, dst) in enumerate((
        (deg_any, deg_ref), (sk_any, sk_ref), (vals_any, vals), (rows_any, rows_ref), (cols_any, cols_ref),
        (live_any, live_ref)))]
    for load in loads:
        load.start()
    barrier = pltpu.get_barrier_semaphore()
    moves = sorted({(wrap(d * m[0], NY), wrap(d * m[1], NZ)) for m in PLAN for d in (1, -1)})
    peers = [(row_of(y + dy, z + dz), col) for dy, dz in moves]
    peers += [(row, lax.rem(col + k, 2 * NX)) for k in range(1, 2 * NX)]
    for peer in peers:
        pl.semaphore_signal(barrier, inc=1, device_id=peer, device_id_type=MESH)
    loads[0].wait()
    loads[1].wait()
    ids_r = lax.broadcasted_iota(jnp.int32, (BLK, BLK), 0)
    ids_c = lax.broadcasted_iota(jnp.int32, (BLK, BLK), 1)
    spread = jnp.where(ids_r == ids_c, jnp.broadcast_to(deg_ref[...], (BLK, BLK)), 0.0)
    scale = lax.rsqrt(jnp.sum(spread, axis=1, keepdims=True))
    gat[y, LOW] = (scale * sk_ref[...].astype(jnp.float32)).astype(jnp.bfloat16)
    pl.semaphore_wait(barrier, len(peers))

    def blocks(oy, oz, count, lo, hi):
        ys = slice(None) if oy is None else lax.rem(y + oy + NY, NY)
        return gat.at[ys, pl.ds(oz + LOW, count), pl.ds(lo, hi - lo), :]

    def message(i):
        dy, dz, oy, oz, count, lo, hi = PLAN[i]
        return pltpu.make_async_remote_copy(
            src_ref=blocks(oy, oz, count, lo, hi), dst_ref=blocks(oy, wrap(oz - dz, NZ), count, lo, hi),
            send_sem=gs.at[i], recv_sem=gr.at[i],
            device_id=(row_of(y + dy, z + dz), col), device_id_type=MESH)

    def landed(i):
        dy, dz, oy, oz, count, lo, hi = PLAN[i]
        block = blocks(None if oy is None else oy - dy, wrap(oz - dz, NZ), count, lo, hi)
        pltpu.make_async_remote_copy(
            src_ref=block, dst_ref=block, send_sem=gs.at[i], recv_sem=gr.at[i],
            device_id=(row_of(y + dy, z + dz), col), device_id_type=MESH).wait_recv()

    def places(oy, oz, count):
        return {(wrap(v, NY), wrap(oz + k, NZ)) for v in (range(NY) if oy is None else (oy,)) for k in range(count)}

    waited = set()
    for i, (_, _, oy, oz, count, lo, hi) in enumerate(PLAN):
        for j, (dy, dz, py, pz, many, plo, phi) in enumerate(PLAN):
            brought = places(None if py is None else py - dy, pz - dz, many)
            if j not in waited and plo < hi and lo < phi and brought & places(oy, oz, count):
                landed(j)
                waited.add(j)
        message(i).start()
    for j in range(N_PLAN):
        if j not in waited:
            landed(j)

    for load in loads[2:]:
        load.wait()
    for s in range(SLOTS):
        at = cols_ref[0, 0, s]
        picked = gat[at // NZ, lax.rem(lax.rem(at, NZ) - z + LOW + NZ, NZ)]
        prods[s] = jnp.dot(vals[s], picked, preferred_element_type=jnp.float32)
    live = live_ref[0, 0]
    for r in range(2 * NX):
        weights = [jnp.where((rows_ref[0, 0, s] == r) & (s < live), 1.0, 0.0) for s in range(SLOTS)]
        for k in range(BLK // 16):
            lines = pl.ds(k * 16, 16)
            total = weights[0] * prods[0, lines, :]
            for s in range(1, SLOTS):
                total = total + weights[s] * prods[s, lines, :]
            part[r % 2, r // 2, lines, :] = total

    other = 1 - core
    swap = pltpu.make_async_remote_copy(
        src_ref=part.at[other], dst_ref=crecv, send_sem=cs, recv_sem=cr,
        device_id=(row, x * 2 + other), device_id_type=MESH)
    swap.start()
    swap.wait_recv()
    sends = []
    for k in (2, 1, 3):
        to = lax.rem(x + k, NX)
        comb[k] = part[core, to] + crecv[to]
        send = pltpu.make_async_remote_copy(
            src_ref=comb.at[k], dst_ref=xrecv.at[k], send_sem=xs.at[k], recv_sem=xr.at[k],
            device_id=(row, to * 2 + core), device_id_type=MESH)
        send.start()
        sends.append(send)
    total = part[core, x] + crecv[x]
    for send in (sends[1], sends[2], sends[0]):
        send.wait_recv()
    for k in (1, 2, 3):
        total = total + xrecv[k]
    image = scale * total
    image_ref[...] = image
    glocal[...] = lax.dot_general(image, image, (((0,), (0,)), ((), ())), precision=HIGHEST,
                                  preferred_element_type=jnp.float32)

    chip = x * NY + y
    me = chip * 2 + core
    keeper = lax.rem(x + y, 2)
    owner = core == keeper

    def plane(t):
        tx, ty = t // NY, lax.rem(t, NY)
        return tx, ty, lax.rem(tx + ty, 2)

    def scatter(k):
        t = lax.rem(chip + k, NX * NY)
        tx, ty, tc = plane(t)
        return pltpu.make_async_remote_copy(
            src_ref=glocal.at[pl.ds(pl.multiple_of(t * 8, 8), 8), :], dst_ref=rsbuf.at[me],
            send_sem=rs_s.at[k], recv_sem=rs_r.at[me],
            device_id=(row_of(ty, z), tx * 2 + tc), device_id_type=MESH)

    for k in list(range(1, NX * NY)):
        scatter(k).start()

    @pl.when(jnp.logical_not(owner))
    def _():
        scatter(0).start()

    mine = pl.ds(pl.multiple_of(chip * 8, 8), 8)

    @pl.when(owner)
    def _():
        total = glocal[mine, :]
        for k in range(1, 2 * NX * NY):
            src = lax.rem(me + k, 2 * NX * NY)
            pltpu.make_async_remote_copy(
                src_ref=rsbuf.at[src], dst_ref=rsbuf.at[src], send_sem=rs_s.at[0], recv_sem=rs_r.at[src],
                device_id=(row, x * 2 + other), device_id_type=MESH).wait_recv()
        for k in range(1, 2 * NX * NY):
            total = total + rsbuf[lax.rem(me + k, 2 * NX * NY)]
        zbuf[z] = total

        def along(k):
            return pltpu.make_async_remote_copy(
                src_ref=zbuf.at[z], dst_ref=zbuf.at[z], send_sem=z_s.at[k], recv_sem=z_r.at[z],
                device_id=(row_of(y, z + k), col), device_id_type=MESH)

        order = sorted(range(1, NZ), key=lambda k: -min(k, NZ - k))
        for k in order:
            along(k).start()
        for k in reversed(order):
            src = lax.rem(z + k, NZ)
            pltpu.make_async_remote_copy(
                src_ref=zbuf.at[src], dst_ref=zbuf.at[src], send_sem=z_s.at[k], recv_sem=z_r.at[src],
                device_id=(row_of(y, z + k), col), device_id_type=MESH).wait_recv()
        total = zbuf[0]
        for k in range(1, NZ):
            total = total + zbuf[k]
        gram_ref[mine, :] = total

        def back(k):
            if k == 0:
                device = (row, x * 2 + other)
            else:
                t = lax.rem(chip + k // 2, NX * NY)
                device = (row_of(lax.rem(t, NY), z), t // NY * 2 + k % 2)
            return pltpu.make_async_remote_copy(
                src_ref=gram_ref.at[mine, :], dst_ref=gram_ref.at[mine, :], send_sem=ag_s.at[k],
                recv_sem=ag_r.at[chip], device_id=device, device_id_type=MESH)

        spots = [0] + list(range(2, 2 * NX * NY))
        for k in spots[::-1]:
            back(k).start()
        for k in order:
            along(k).wait_send()
        for k in spots:
            back(k).wait_send()

    def arrive(t):
        lines = pl.ds(pl.multiple_of(t * 8, 8), 8)
        pltpu.make_async_remote_copy(
            src_ref=gram_ref.at[lines, :], dst_ref=gram_ref.at[lines, :], send_sem=ag_s.at[0],
            recv_sem=ag_r.at[t], device_id=(row, x * 2 + other), device_id_type=MESH).wait_recv()

    for k in range(1, NX * NY):
        arrive(lax.rem(chip + k, NX * NY))

    @pl.when(jnp.logical_not(owner))
    def _():
        arrive(chip)
        scatter(0).wait_send()

    for i in range(N_PLAN):
        message(i).wait_send()
    swap.wait_send()
    for send in sends:
        send.wait_send()
    for k in range(1, NX * NY):
        scatter(k).wait_send()


def factor_kernel(nodes, gram_ref, image_ref, basis_ref, factor_ref, inv_ref):
    tiles = BLK // 8
    left = [gram_ref[pl.ds(k * 8, 8), :] * (1.0 / nodes) for k in range(tiles)]
    row_ids = lax.broadcasted_iota(jnp.int32, (8, BLK), 0)
    lane_ids = lax.broadcasted_iota(jnp.int32, (8, BLK), 1)
    right = [jnp.where(row_ids + 8 * k == lane_ids, 1.0, 0.0) for k in range(tiles)]
    for j in range(BLK):
        k0, r = divmod(j, 8)
        pivot = left[k0][r:r + 1, j:j + 1]
        inv = lax.rsqrt(pivot)
        up_left = left[k0][r:r + 1, :] * inv
        up_right = right[k0][r:r + 1, :] * inv
        factor_ref[pl.ds(j, 1), :] = jnp.where(lane_ids[:1] >= j, up_left, 0.0)
        inv_ref[pl.ds(j, 1), :] = up_right
        for k in range(k0, tiles):
            by = left[k][:, j:j + 1] * inv
            if k == k0:
                if r == 7:
                    continue
                by = jnp.where(row_ids[:, :1] > r, by, 0.0)
            left[k] = left[k] - by * up_left
            right[k] = right[k] - by * up_right
    basis_ref[...] = lax.dot_general(image_ref[...], inv_ref[...], (((1,), (1,)), ((), ())), precision=HIGHEST,
                                     preferred_element_type=jnp.float32)


def local(sketch, degree, block_vals, block_rows, block_cols, live_count):
    f32 = jnp.float32
    square = jax.ShapeDtypeStruct((BLK, BLK), f32)
    vmem = pl.BlockSpec(memory_space=pltpu.VMEM)
    dma = pltpu.SemaphoreType.DMA
    gram, image = pl.pallas_call(
        comm_kernel,
        out_shape=(square, square),
        in_specs=[pl.BlockSpec(memory_space=pl.ANY)] * 6,
        out_specs=(vmem, vmem),
        scratch_shapes=[
            pltpu.VMEM((BLK, BLK), jnp.bfloat16),
            pltpu.VMEM((1, BLK), f32),
            pltpu.SMEM((1, 1, SLOTS), jnp.int32),
            pltpu.SMEM((1, 1, SLOTS), jnp.int32),
            pltpu.SMEM((1, 1), jnp.int32),
            pltpu.VMEM((NY, NZ, BLK, BLK), jnp.bfloat16),
            pltpu.VMEM((SLOTS, BLK, BLK), jnp.bfloat16),
            pltpu.VMEM((SLOTS, BLK, BLK), f32),
            pltpu.VMEM((2, NX, BLK, BLK), f32),
            pltpu.VMEM((NX, BLK, BLK), f32),
            pltpu.VMEM((NX, BLK, BLK), f32),
            pltpu.VMEM((NX, BLK, BLK), f32),
            pltpu.VMEM((BLK, BLK), f32),
            pltpu.VMEM((2 * NX * NY, 8, BLK), f32),
            pltpu.VMEM((NZ, 8, BLK), f32),
            dma((6,)), dma((N_PLAN,)), dma((N_PLAN,)), dma, dma, dma((NX,)), dma((NX,)),
            dma((NX * NY,)), dma((2 * NX * NY,)), dma((NZ,)), dma((NZ,)), dma((2 * NX * NY,)), dma((NX * NY,)),
        ],
        compiler_params=pltpu.CompilerParams(collective_id=0, has_side_effects=True),
        name="spread",
    )(sketch, degree.reshape(1, BLK), block_vals.reshape(SLOTS, BLK, BLK), block_rows, block_cols,
      live_count)
    nodes = BLK * lax.axis_size("row") * lax.axis_size("col")
    return pl.pallas_call(
        functools.partial(factor_kernel, nodes),
        out_shape=(square, square),
        in_specs=[vmem, vmem],
        out_specs=(vmem, vmem),
        scratch_shapes=[pltpu.VMEM((BLK, BLK), f32)],
        name="orthonormalize",
    )(gram, image)


def solution(mesh):
    in_specs = (
        P(("row", "col"), None),
        P(("row", "col")),
        P("row", "col", None, None, None),
        P("row", "col", None),
        P("row", "col", None),
        P("row", "col"),
    )
    out_specs = (P(("row", "col"), None), P())
    return jax.shard_map(local, mesh=mesh, in_specs=in_specs, out_specs=out_specs, check_vma=False)
```

```python
import functools

import jax
import jax.numpy as jnp
from jax import lax
from jax.experimental import pallas as pl
from jax.experimental.pallas import tpu as pltpu
from jax.sharding import PartitionSpec as P

MESH = pl.DeviceIdType.MESH
HIGHEST = lax.Precision.HIGHEST
NX, NY, NZ = 4, 4, 16
BLK = 128
SLOTS = 16

PLAN = (
    (1, 0, 0, 0, 1, 96, 128),
    (-1, 0, 0, 0, 1, 96, 128),
    (0, 3, 0, 0, 1, 0, 96),
    (0, -3, 0, 0, 1, 0, 96),
    (0, 1, 0, 0, 1, 0, 96),
    (0, -1, 0, 0, 1, 0, 96),
    (1, 0, 0, 0, 1, 0, 96),
    (-1, 0, 0, 0, 1, 0, 96),
    (1, 0, -1, 0, 1, 96, 112),
    (-1, 0, 1, 0, 1, 112, 128),
    (1, 0, -1, 0, 1, 0, 48),
    (-1, 0, 1, 0, 1, 48, 96),
    (0, 3, 0, -3, 1, 0, 96),
    (0, -3, 0, 3, 1, 0, 96),
    (0, -1, 0, -3, 1, 0, 96),
    (0, 1, 0, -3, 1, 0, 96),
    (0, 3, None, 0, 1, 96, 128),
    (0, -3, None, 0, 1, 96, 128),
    (0, 1, 0, 3, 1, 0, 96),
    (0, -1, 0, 3, 1, 0, 96),
    (1, 0, 0, 1, 1, 0, 96),
    (-1, 0, 0, 1, 1, 0, 96),
    (1, 0, 0, -1, 1, 0, 96),
    (-1, 0, 0, -1, 1, 0, 96),
    (0, 1, None, 0, 1, 96, 128),
    (0, -1, None, 0, 1, 96, 128),
    (0, 1, 0, -6, 1, 0, 96),
    (0, -1, 0, 6, 1, 0, 96),
    (0, -1, 0, -6, 1, 0, 96),
    (0, 1, 0, 6, 1, 0, 96),
    (1, 0, 0, -3, 2, 0, 96),
    (-1, 0, 0, -3, 2, 0, 96),
    (1, 0, -1, 1, 1, 0, 48),
    (-1, 0, 1, 1, 1, 48, 96),
    (1, 0, -1, -1, 1, 0, 48),
    (-1, 0, 1, -1, 1, 48, 96),
    (0, 3, None, -3, 1, 96, 128),
    (0, -3, None, 3, 1, 96, 128),
    (0, -1, None, -3, 1, 96, 128),
    (0, 1, None, -3, 1, 96, 128),
    (0, 1, None, 3, 1, 96, 128),
    (1, 0, 0, 2, 2, 0, 96),
    (-1, 0, 0, 2, 2, 0, 96),
    (0, -1, None, 3, 1, 96, 128),
    (1, 0, -1, -3, 2, 0, 48),
    (-1, 0, 1, -3, 2, 48, 96),
    (0, 1, 0, -7, 1, 0, 48),
    (0, -1, 0, 7, 1, 48, 96),
    (1, 0, 0, 6, 2, 0, 96),
    (-1, 0, 0, 6, 2, 0, 96),
    (1, 0, 0, 4, 2, 0, 96),
    (-1, 0, 0, 4, 2, 0, 96),
    (1, 0, 0, -5, 2, 0, 96),
    (-1, 0, 0, -5, 2, 0, 96),
    (1, 0, 0, -7, 2, 0, 96),
    (-1, 0, 0, -7, 2, 0, 96),
    (1, 0, -1, 2, 2, 0, 48),
    (-1, 0, 1, 2, 2, 48, 96),
    (0, 1, None, -6, 1, 96, 128),
    (0, -1, None, 6, 1, 96, 128),
    (0, -1, None, -6, 1, 96, 128),
    (0, 1, None, 6, 1, 96, 128),
    (1, 0, -1, 6, 2, 0, 48),
    (-1, 0, 1, 6, 2, 48, 96),
    (1, 0, 0, 8, 1, 0, 96),
    (-1, 0, 0, 8, 1, 0, 96),
    (1, 0, -1, 4, 2, 0, 48),
    (-1, 0, 1, 4, 2, 48, 96),
    (0, 1, None, -7, 1, 96, 112),
    (0, -1, None, 7, 1, 112, 128),
    (1, 0, -1, -5, 2, 0, 48),
    (-1, 0, 1, -5, 2, 48, 96),
    (1, 0, -1, -7, 2, 0, 48),
    (-1, 0, 1, -7, 2, 48, 96),
    (1, 0, -1, 8, 1, 0, 48),
    (-1, 0, 1, 8, 1, 48, 96),
)
N_PLAN = len(PLAN)
LOW = NZ // 2 - 1


def wrap(value, n):
    value = value % n
    return value - n if value > n // 2 else value


def row_of(y, z):
    return lax.rem(y + 4 * NY, NY) * NZ + lax.rem(z + 4 * NZ, NZ)


def comm_kernel(sk_any, deg_any, vals_any, rows_any, cols_any, live_any, gram_ref, image_ref,
                sk_ref, deg_ref, rows_ref, cols_ref, live_ref, gat, vals, prods, part, crecv, comb, xrecv, glocal, rsbuf, zbuf,
                vsem, gs, gr, cs, cr, xs, xr, rs_s, rs_r, z_s, z_r, ag_s, ag_r):
    row = lax.axis_index("row")
    col = lax.axis_index("col")
    y, z = row // NZ, lax.rem(row, NZ)
    x, core = col // 2, lax.rem(col, 2)

    loads = [pltpu.make_async_copy(src, dst, vsem.at[i]) for i, (src, dst) in enumerate((
        (deg_any, deg_ref), (sk_any, sk_ref), (vals_any, vals), (rows_any, rows_ref), (cols_any, cols_ref),
        (live_any, live_ref)))]
    for load in loads:
        load.start()
    barrier = pltpu.get_barrier_semaphore()
    moves = sorted({(wrap(d * m[0], NY), wrap(d * m[1], NZ)) for m in PLAN for d in (1, -1)})
    peers = [(row_of(y + dy, z + dz), col) for dy, dz in moves]
    peers += [(row, lax.rem(col + k, 2 * NX)) for k in range(1, 2 * NX)]
    for peer in peers:
        pl.semaphore_signal(barrier, inc=1, device_id=peer, device_id_type=MESH)
    loads[0].wait()
    loads[1].wait()
    ids_r = lax.broadcasted_iota(jnp.int32, (BLK, BLK), 0)
    ids_c = lax.broadcasted_iota(jnp.int32, (BLK, BLK), 1)
    spread = jnp.where(ids_r == ids_c, jnp.broadcast_to(deg_ref[...], (BLK, BLK)), 0.0)
    scale = lax.rsqrt(jnp.sum(spread, axis=1, keepdims=True))
    gat[y, LOW] = (scale * sk_ref[...].astype(jnp.float32)).astype(jnp.bfloat16)
    pl.semaphore_wait(barrier, len(peers))

    def blocks(oy, oz, count, lo, hi):
        ys = slice(None) if oy is None else lax.rem(y + oy + NY, NY)
        return gat.at[ys, pl.ds(oz + LOW, count), pl.ds(lo, hi - lo), :]

    def message(i):
        dy, dz, oy, oz, count, lo, hi = PLAN[i]
        return pltpu.make_async_remote_copy(
            src_ref=blocks(oy, oz, count, lo, hi), dst_ref=blocks(oy, wrap(oz - dz, NZ), count, lo, hi),
            send_sem=gs.at[i], recv_sem=gr.at[i],
            device_id=(row_of(y + dy, z + dz), col), device_id_type=MESH)

    def landed(i):
        dy, dz, oy, oz, count, lo, hi = PLAN[i]
        block = blocks(None if oy is None else oy - dy, wrap(oz - dz, NZ), count, lo, hi)
        pltpu.make_async_remote_copy(
            src_ref=block, dst_ref=block, send_sem=gs.at[i], recv_sem=gr.at[i],
            device_id=(row_of(y + dy, z + dz), col), device_id_type=MESH).wait_recv()

    def places(oy, oz, count):
        return {(wrap(v, NY), wrap(oz + k, NZ)) for v in (range(NY) if oy is None else (oy,)) for k in range(count)}

    waited = set()
    for i, (_, _, oy, oz, count, lo, hi) in enumerate(PLAN):
        for j, (dy, dz, py, pz, many, plo, phi) in enumerate(PLAN):
            brought = places(None if py is None else py - dy, pz - dz, many)
            if j not in waited and plo < hi and lo < phi and brought & places(oy, oz, count):
                landed(j)
                waited.add(j)
        message(i).start()
    for j in range(N_PLAN):
        if j not in waited:
            landed(j)

    for load in loads[2:]:
        load.wait()
    for s in range(SLOTS):
        at = cols_ref[0, 0, s]
        picked = gat[at // NZ, lax.rem(lax.rem(at, NZ) - z + LOW + NZ, NZ)]
        prods[s] = jnp.dot(vals[s], picked, preferred_element_type=jnp.float32)
    live = live_ref[0, 0]
    for r in range(2 * NX):
        weights = [jnp.where((rows_ref[0, 0, s] == r) & (s < live), 1.0, 0.0) for s in range(SLOTS)]
        for k in range(BLK // 16):
            lines = pl.ds(k * 16, 16)
            total = weights[0] * prods[0, lines, :]
            for s in range(1, SLOTS):
                total = total + weights[s] * prods[s, lines, :]
            part[r % 2, r // 2, lines, :] = total

    other = 1 - core
    swap = pltpu.make_async_remote_copy(
        src_ref=part.at[other], dst_ref=crecv, send_sem=cs, recv_sem=cr,
        device_id=(row, x * 2 + other), device_id_type=MESH)
    swap.start()
    swap.wait_recv()
    sends = []
    for k in (2, 1, 3):
        to = lax.rem(x + k, NX)
        comb[k] = part[core, to] + crecv[to]
        send = pltpu.make_async_remote_copy(
            src_ref=comb.at[k], dst_ref=xrecv.at[k], send_sem=xs.at[k], recv_sem=xr.at[k],
            device_id=(row, to * 2 + core), device_id_type=MESH)
        send.start()
        sends.append(send)
    total = part[core, x] + crecv[x]
    for send in (sends[1], sends[2], sends[0]):
        send.wait_recv()
    for k in (1, 2, 3):
        total = total + xrecv[k]
    image = scale * total
    image_ref[...] = image
    glocal[...] = lax.dot_general(image, image, (((0,), (0,)), ((), ())), precision=HIGHEST,
                                  preferred_element_type=jnp.float32)

    chip = x * NY + y
    me = chip * 2 + core
    keeper = lax.rem(x + y, 2)
    owner = core == keeper

    def plane(t):
        tx, ty = t // NY, lax.rem(t, NY)
        return tx, ty, lax.rem(tx + ty, 2)

    def scatter(k):
        t = lax.rem(chip + k, NX * NY)
        tx, ty, tc = plane(t)
        return pltpu.make_async_remote_copy(
            src_ref=glocal.at[pl.ds(pl.multiple_of(t * 8, 8), 8), :], dst_ref=rsbuf.at[me],
            send_sem=rs_s.at[k], recv_sem=rs_r.at[me],
            device_id=(row_of(ty, z), tx * 2 + tc), device_id_type=MESH)

    for k in list(range(1, NX * NY)):
        scatter(k).start()

    @pl.when(jnp.logical_not(owner))
    def _():
        scatter(0).start()

    mine = pl.ds(pl.multiple_of(chip * 8, 8), 8)

    @pl.when(owner)
    def _():
        total = glocal[mine, :]
        for k in range(1, 2 * NX * NY):
            src = lax.rem(me + k, 2 * NX * NY)
            pltpu.make_async_remote_copy(
                src_ref=rsbuf.at[src], dst_ref=rsbuf.at[src], send_sem=rs_s.at[0], recv_sem=rs_r.at[src],
                device_id=(row, x * 2 + other), device_id_type=MESH).wait_recv()
        for k in range(1, 2 * NX * NY):
            total = total + rsbuf[lax.rem(me + k, 2 * NX * NY)]
        zbuf[z] = total

        def along(k):
            return pltpu.make_async_remote_copy(
                src_ref=zbuf.at[z], dst_ref=zbuf.at[z], send_sem=z_s.at[k], recv_sem=z_r.at[z],
                device_id=(row_of(y, z + k), col), device_id_type=MESH)

        order = sorted(range(1, NZ), key=lambda k: -min(k, NZ - k))
        for k in order:
            along(k).start()
        for k in reversed(order):
            src = lax.rem(z + k, NZ)
            pltpu.make_async_remote_copy(
                src_ref=zbuf.at[src], dst_ref=zbuf.at[src], send_sem=z_s.at[k], recv_sem=z_r.at[src],
                device_id=(row_of(y, z + k), col), device_id_type=MESH).wait_recv()
        total = zbuf[0]
        for k in range(1, NZ):
            total = total + zbuf[k]
        gram_ref[mine, :] = total

        def back(k):
            if k == 0:
                device = (row, x * 2 + other)
            else:
                t = lax.rem(chip + k // 2, NX * NY)
                device = (row_of(lax.rem(t, NY), z), t // NY * 2 + k % 2)
            return pltpu.make_async_remote_copy(
                src_ref=gram_ref.at[mine, :], dst_ref=gram_ref.at[mine, :], send_sem=ag_s.at[k],
                recv_sem=ag_r.at[chip], device_id=device, device_id_type=MESH)

        spots = [0] + list(range(2, 2 * NX * NY))
        for k in spots[::-1]:
            back(k).start()
        for k in order:
            along(k).wait_send()
        for k in spots:
            back(k).wait_send()

    def arrive(t):
        lines = pl.ds(pl.multiple_of(t * 8, 8), 8)
        pltpu.make_async_remote_copy(
            src_ref=gram_ref.at[lines, :], dst_ref=gram_ref.at[lines, :], send_sem=ag_s.at[0],
            recv_sem=ag_r.at[t], device_id=(row, x * 2 + other), device_id_type=MESH).wait_recv()

    for k in range(1, NX * NY):
        arrive(lax.rem(chip + k, NX * NY))

    @pl.when(jnp.logical_not(owner))
    def _():
        arrive(chip)
        scatter(0).wait_send()

    for i in range(N_PLAN):
        message(i).wait_send()
    swap.wait_send()
    for send in sends:
        send.wait_send()
    for k in range(1, NX * NY):
        scatter(k).wait_send()


def factor_kernel(nodes, gram_ref, image_ref, basis_ref, factor_ref, inv_ref):
    tiles = BLK // 8
    full = (8, BLK)
    left = [gram_ref[pl.ds(k * 8, 8), :] * (1.0 / nodes) for k in range(tiles)]
    row_ids = lax.broadcasted_iota(jnp.int32, full, 0)
    lane_ids = lax.broadcasted_iota(jnp.int32, full, 1)
    right = [jnp.where(row_ids + 8 * k == lane_ids, 1.0, 0.0) for k in range(tiles)]
    for t in range(tiles):
        base = t * 8
        lrow = [jnp.broadcast_to(left[t][r:r + 1, :], full) for r in range(8)]
        rrow = [jnp.broadcast_to(right[t][r:r + 1, :], full) for r in range(8)]
        entry = {(i, j): jnp.broadcast_to(lrow[i][:, base + j:base + j + 1], full) for i in range(8) for j in range(i, 8)}
        mult = {}
        recip = []
        for j in range(8):
            root = lax.rsqrt(entry[j, j])
            inv = root * root
            recip.append(inv)
            pairs = {(i, k): entry[j, i] * entry[j, k] for i in range(j + 1, 8) for k in range(i, 8)}
            for i, k in pairs:
                entry[i, k] = entry[i, k] - pairs[i, k] * inv
            for i in range(j + 1, 8):
                mult[i, j] = entry[j, i] * inv
                lrow[i] = lrow[i] - mult[i, j] * lrow[j]
                rrow[i] = rrow[i] - mult[i, j] * rrow[j]
            factor_ref[pl.ds(base + j, 1), :] = jnp.where(lane_ids[:1] >= base + j, (lrow[j] * root)[:1], 0.0)
            inv_ref[pl.ds(base + j, 1), :] = (rrow[j] * root)[:1]
        if t == tiles - 1:
            break
        for j in range(7, -1, -1):
            lrow[j] = lrow[j] * recip[j]
            rrow[j] = rrow[j] * recip[j]
            for i in range(7, j, -1):
                lrow[j] = lrow[j] - mult[i, j] * lrow[i]
                rrow[j] = rrow[j] - mult[i, j] * rrow[i]
        for k in range(t + 1, tiles):
            old = left[k]
            for j in range(7, -1, -1):
                by = jnp.broadcast_to(old[:, base + j:base + j + 1], full)
                left[k] = left[k] - by * lrow[j]
                right[k] = right[k] - by * rrow[j]
    basis_ref[...] = lax.dot_general(image_ref[...], inv_ref[...], (((1,), (1,)), ((), ())), precision=HIGHEST,
                                     preferred_element_type=jnp.float32)


def local(sketch, degree, block_vals, block_rows, block_cols, live_count):
    f32 = jnp.float32
    square = jax.ShapeDtypeStruct((BLK, BLK), f32)
    vmem = pl.BlockSpec(memory_space=pltpu.VMEM)
    dma = pltpu.SemaphoreType.DMA
    gram, image = pl.pallas_call(
        comm_kernel,
        out_shape=(pltpu.VMEM((BLK, BLK), f32), pltpu.VMEM((BLK, BLK), f32)),
        in_specs=[pl.BlockSpec(memory_space=pl.ANY)] * 6,
        out_specs=(vmem, vmem),
        scratch_shapes=[
            pltpu.VMEM((BLK, BLK), jnp.bfloat16),
            pltpu.VMEM((1, BLK), f32),
            pltpu.SMEM((1, 1, SLOTS), jnp.int32),
            pltpu.SMEM((1, 1, SLOTS), jnp.int32),
            pltpu.SMEM((1, 1), jnp.int32),
            pltpu.VMEM((NY, NZ, BLK, BLK), jnp.bfloat16),
            pltpu.VMEM((SLOTS, BLK, BLK), jnp.bfloat16),
            pltpu.VMEM((SLOTS, BLK, BLK), f32),
            pltpu.VMEM((2, NX, BLK, BLK), f32),
            pltpu.VMEM((NX, BLK, BLK), f32),
            pltpu.VMEM((NX, BLK, BLK), f32),
            pltpu.VMEM((NX, BLK, BLK), f32),
            pltpu.VMEM((BLK, BLK), f32),
            pltpu.VMEM((2 * NX * NY, 8, BLK), f32),
            pltpu.VMEM((NZ, 8, BLK), f32),
            dma((6,)), dma((N_PLAN,)), dma((N_PLAN,)), dma, dma, dma((NX,)), dma((NX,)),
            dma((NX * NY,)), dma((2 * NX * NY,)), dma((NZ,)), dma((NZ,)), dma((2 * NX * NY,)), dma((NX * NY,)),
        ],
        compiler_params=pltpu.CompilerParams(collective_id=0, has_side_effects=True),
        name="spread",
    )(sketch, degree.reshape(1, BLK), block_vals.reshape(SLOTS, BLK, BLK), block_rows, block_cols,
      live_count)
    gram = pltpu.with_memory_space_constraint(gram, pltpu.VMEM)
    image = pltpu.with_memory_space_constraint(image, pltpu.VMEM)
    nodes = BLK * lax.axis_size("row") * lax.axis_size("col")
    return pl.pallas_call(
        functools.partial(factor_kernel, nodes),
        out_shape=(square, square),
        in_specs=[vmem, vmem],
        out_specs=(vmem, vmem),
        scratch_shapes=[pltpu.VMEM((BLK, BLK), f32)],
        name="orthonormalize",
    )(gram, image)


def solution(mesh):
    in_specs = (
        P(("row", "col"), None),
        P(("row", "col")),
        P("row", "col", None, None, None),
        P("row", "col", None),
        P("row", "col", None),
        P("row", "col"),
    )
    out_specs = (P(("row", "col"), None), P())
    return jax.shard_map(local, mesh=mesh, in_specs=in_specs, out_specs=out_specs, check_vma=False)
```

```python
import functools

import jax
import jax.numpy as jnp
from jax import lax
from jax.experimental import pallas as pl
from jax.experimental.pallas import tpu as pltpu
from jax.sharding import PartitionSpec as P

MESH = pl.DeviceIdType.MESH
HIGHEST = lax.Precision.HIGHEST
NX, NY, NZ = 4, 4, 16
BLK = 128
SLOTS = 16

PLAN = (
    (0, 1, 0, 0, 1, 0, 96),
    (0, -1, 0, 0, 1, 0, 96),
    (2, 0, 0, 0, 1, 96, 112),
    (-2, 0, 0, 0, 1, 112, 128),
    (0, 3, 0, 0, 1, 0, 96),
    (0, -3, 0, 0, 1, 0, 96),
    (1, 0, 0, 0, 1, 96, 128),
    (-1, 0, 0, 0, 1, 96, 128),
    (1, 0, 0, 0, 1, 0, 96),
    (-1, 0, 0, 0, 1, 0, 96),
    (0, 1, 0, -1, 1, 0, 96),
    (0, -1, 0, 1, 1, 0, 96),
    (2, 0, 0, 1, 1, 0, 48),
    (0, 1, None, 0, 1, 96, 128),
    (0, -1, None, 0, 1, 96, 128),
    (-2, 0, 0, 1, 1, 48, 96),
    (2, 0, 0, -1, 1, 0, 48),
    (-2, 0, 0, -1, 1, 48, 96),
    (0, 2, 0, -3, 1, 0, 96),
    (0, -2, 0, 3, 1, 0, 96),
    (1, 0, 0, 1, 1, 0, 96),
    (-1, 0, 0, 1, 1, 0, 96),
    (1, 0, 0, -1, 1, 0, 96),
    (0, 2, 0, -2, 1, 0, 96),
    (0, -2, 0, 2, 1, 0, 96),
    (1, 0, 0, 2, 2, 0, 96),
    (-1, 0, 0, 2, 2, 0, 96),
    (0, 2, None, -1, 1, 96, 128),
    (1, 0, 0, -3, 2, 0, 96),
    (0, -2, None, 1, 1, 96, 128),
    (-1, 0, 0, -3, 2, 0, 96),
    (-1, 0, 0, -1, 1, 0, 96),
    (1, 0, -1, 0, 1, 0, 48),
    (-1, 0, 1, 0, 1, 48, 96),
    (0, 3, 0, -5, 1, 0, 48),
    (0, -3, 0, 5, 1, 48, 96),
    (0, 2, 0, -5, 1, 0, 96),
    (0, -2, 0, 5, 1, 0, 96),
    (0, 2, 0, -4, 1, 0, 96),
    (0, -2, 0, 4, 1, 0, 96),
    (1, 0, 0, 4, 2, 0, 96),
    (-1, 0, 0, 4, 2, 0, 96),
    (1, 0, 0, -5, 2, 0, 96),
    (-1, 0, 0, -5, 2, 0, 96),
    (0, 2, None, -3, 1, 96, 128),
    (0, -2, None, 3, 1, 96, 128),
    (0, -1, None, -3, 1, 96, 128),
    (0, 1, None, 3, 1, 96, 128),
    (0, 1, None, -3, 1, 96, 128),
    (0, -1, None, 3, 1, 96, 128),
    (1, 0, -1, 2, 2, 0, 48),
    (-1, 0, 1, 2, 2, 48, 96),
    (1, 0, -1, -3, 2, 0, 48),
    (1, 0, 0, 8, 1, 0, 96),
    (-1, 0, 0, 8, 1, 0, 96),
    (1, 0, 0, 7, 1, 0, 96),
    (-1, 0, 0, 7, 1, 0, 96),
    (1, 0, 0, -7, 1, 0, 96),
    (-1, 0, 0, -7, 1, 0, 96),
    (-1, 0, 1, -3, 2, 48, 96),
    (1, 0, 0, -6, 1, 0, 96),
    (1, 0, 0, 6, 1, 0, 96),
    (-1, 0, 0, 6, 1, 0, 96),
    (-1, 0, 0, -6, 1, 0, 96),
    (1, 0, -1, 4, 2, 0, 48),
    (-1, 0, 1, 4, 2, 48, 96),
    (1, 0, -1, -5, 2, 0, 48),
    (0, 3, None, -5, 1, 96, 112),
    (0, -3, None, 5, 1, 112, 128),
    (0, 2, None, -5, 1, 96, 128),
    (0, -2, None, 5, 1, 96, 128),
    (0, 1, None, -5, 1, 96, 128),
    (0, -1, None, 5, 1, 96, 128),
    (-1, 0, 1, -5, 2, 48, 96),
    (1, 0, -1, 7, 1, 0, 48),
    (-1, 0, 1, 7, 1, 48, 96),
    (1, 0, -1, -7, 1, 0, 48),
    (-1, 0, 1, -7, 1, 48, 96),
    (1, 0, -1, 8, 1, 0, 48),
    (1, 0, -1, -6, 1, 0, 48),
    (-1, 0, 1, 6, 1, 48, 96),
    (-1, 0, 1, 8, 1, 48, 96),
    (1, 0, -1, 6, 1, 0, 48),
    (-1, 0, 1, -6, 1, 48, 96),
)
N_PLAN = len(PLAN)
LOW = NZ // 2 - 1


def wrap(value, n):
    value = value % n
    return value - n if value > n // 2 else value


def row_of(y, z):
    return lax.rem(y + 4 * NY, NY) * NZ + lax.rem(z + 4 * NZ, NZ)


def comm_kernel(sk_any, deg_any, vals_any, rows_any, cols_any, live_any, gram_ref, image_ref,
                sk_ref, deg_ref, rows_ref, cols_ref, live_ref, gat, vals, prods, part, crecv, comb, xrecv, glocal, rsbuf, zbuf,
                vsem, gs, gr, cs, cr, xs, xr, rs_s, rs_r, z_s, z_r, ag_s, ag_r):
    row = lax.axis_index("row")
    col = lax.axis_index("col")
    y, z = row // NZ, lax.rem(row, NZ)
    x, core = col // 2, lax.rem(col, 2)

    loads = [pltpu.make_async_copy(src, dst, vsem.at[i]) for i, (src, dst) in enumerate((
        (deg_any, deg_ref), (sk_any, sk_ref), (vals_any, vals), (rows_any, rows_ref), (cols_any, cols_ref),
        (live_any, live_ref)))]
    for load in loads:
        load.start()
    barrier = pltpu.get_barrier_semaphore()
    moves = sorted({(wrap(d * m[0], NY), wrap(d * m[1], NZ)) for m in PLAN for d in (1, -1)})
    peers = [(row_of(y + dy, z + dz), col) for dy, dz in moves]
    peers += [(row, lax.rem(col + k, 2 * NX)) for k in range(1, 2 * NX)]
    for peer in peers:
        pl.semaphore_signal(barrier, inc=1, device_id=peer, device_id_type=MESH)
    loads[0].wait()
    loads[1].wait()
    ids_r = lax.broadcasted_iota(jnp.int32, (BLK, BLK), 0)
    ids_c = lax.broadcasted_iota(jnp.int32, (BLK, BLK), 1)
    spread = jnp.where(ids_r == ids_c, jnp.broadcast_to(deg_ref[...], (BLK, BLK)), 0.0)
    scale = lax.rsqrt(jnp.sum(spread, axis=1, keepdims=True))
    gat[y, LOW] = (scale * sk_ref[...].astype(jnp.float32)).astype(jnp.bfloat16)
    pl.semaphore_wait(barrier, len(peers))

    def blocks(oy, oz, count, lo, hi):
        ys = slice(None) if oy is None else lax.rem(y + oy + NY, NY)
        return gat.at[ys, pl.ds(oz + LOW, count), pl.ds(lo, hi - lo), :]

    def message(i):
        dy, dz, oy, oz, count, lo, hi = PLAN[i]
        return pltpu.make_async_remote_copy(
            src_ref=blocks(oy, oz, count, lo, hi), dst_ref=blocks(oy, wrap(oz - dz, NZ), count, lo, hi),
            send_sem=gs.at[i], recv_sem=gr.at[i],
            device_id=(row_of(y + dy, z + dz), col), device_id_type=MESH)

    def landed(i):
        dy, dz, oy, oz, count, lo, hi = PLAN[i]
        block = blocks(None if oy is None else oy - dy, wrap(oz - dz, NZ), count, lo, hi)
        pltpu.make_async_remote_copy(
            src_ref=block, dst_ref=block, send_sem=gs.at[i], recv_sem=gr.at[i],
            device_id=(row_of(y + dy, z + dz), col), device_id_type=MESH).wait_recv()

    def places(oy, oz, count):
        return {(wrap(v, NY), wrap(oz + k, NZ)) for v in (range(NY) if oy is None else (oy,)) for k in range(count)}

    waited = set()
    for i, (_, _, oy, oz, count, lo, hi) in enumerate(PLAN):
        for j, (dy, dz, py, pz, many, plo, phi) in enumerate(PLAN):
            brought = places(None if py is None else py - dy, pz - dz, many)
            if j not in waited and plo < hi and lo < phi and brought & places(oy, oz, count):
                landed(j)
                waited.add(j)
        message(i).start()
    for j in range(N_PLAN):
        if j not in waited:
            landed(j)

    for load in loads[2:]:
        load.wait()
    for s in range(SLOTS):
        at = cols_ref[0, 0, s]
        picked = gat[at // NZ, lax.rem(lax.rem(at, NZ) - z + LOW + NZ, NZ)]
        prods[s] = jnp.dot(vals[s], picked, preferred_element_type=jnp.float32)
    live = live_ref[0, 0]
    for r in range(2 * NX):
        weights = [jnp.where((rows_ref[0, 0, s] == r) & (s < live), 1.0, 0.0) for s in range(SLOTS)]
        for k in range(BLK // 16):
            lines = pl.ds(k * 16, 16)
            total = weights[0] * prods[0, lines, :]
            for s in range(1, SLOTS):
                total = total + weights[s] * prods[s, lines, :]
            part[r % 2, r // 2, lines, :] = total

    other = 1 - core
    swap = pltpu.make_async_remote_copy(
        src_ref=part.at[other], dst_ref=crecv, send_sem=cs, recv_sem=cr,
        device_id=(row, x * 2 + other), device_id_type=MESH)
    swap.start()
    swap.wait_recv()
    sends = []
    for k in (2, 1, 3):
        to = lax.rem(x + k, NX)
        comb[k] = part[core, to] + crecv[to]
        send = pltpu.make_async_remote_copy(
            src_ref=comb.at[k], dst_ref=xrecv.at[k], send_sem=xs.at[k], recv_sem=xr.at[k],
            device_id=(row, to * 2 + core), device_id_type=MESH)
        send.start()
        sends.append(send)
    total = part[core, x] + crecv[x]
    for send in (sends[1], sends[2], sends[0]):
        send.wait_recv()
    for k in (1, 2, 3):
        total = total + xrecv[k]
    image = scale * total
    image_ref[...] = image
    glocal[...] = lax.dot_general(image, image, (((0,), (0,)), ((), ())), precision=HIGHEST,
                                  preferred_element_type=jnp.float32)

    chip = x * NY + y
    owner = core == lax.rem(x + y, 2)
    spots = sorted(((dx, dy) for dx in range(NX) for dy in range(NY)),
                   key=lambda d: -min(d[0], NX - d[0]) - min(d[1], NY - d[1]))

    def tile_of(tx, ty):
        return pl.ds(pl.multiple_of((tx * NY + ty) * 8, 8), 8)

    def scatter(dx, dy):
        tx, ty = lax.rem(x + dx, NX), lax.rem(y + dy, NY)
        slot = (dx * NY + dy) * 2 + core
        return pltpu.make_async_remote_copy(
            src_ref=glocal.at[tile_of(tx, ty), :], dst_ref=rsbuf.at[slot],
            send_sem=rs_s.at[dx * NY + dy], recv_sem=rs_r.at[slot],
            device_id=(row_of(ty, z), tx * 2 + lax.rem(tx + ty, 2)), device_id_type=MESH)

    for dx, dy in spots[:-1]:
        scatter(dx, dy).start()

    @pl.when(jnp.logical_not(owner))
    def _():
        scatter(0, 0).start()

    mine = tile_of(x, y)

    def collect(slot):
        pltpu.make_async_remote_copy(
            src_ref=rsbuf.at[slot], dst_ref=rsbuf.at[slot], send_sem=rs_s.at[0], recv_sem=rs_r.at[slot],
            device_id=(row, x * 2 + other), device_id_type=MESH).wait_recv()

    @pl.when(owner)
    def _():
        collect(other)
        total = glocal[mine, :] + rsbuf[other]
        for dx, dy in spots[-2::-1]:
            for c in (0, 1):
                collect((dx * NY + dy) * 2 + c)
                total = total + rsbuf[(dx * NY + dy) * 2 + c]
        zbuf[z] = total

        def along(k):
            return pltpu.make_async_remote_copy(
                src_ref=zbuf.at[z], dst_ref=zbuf.at[z], send_sem=z_s.at[k], recv_sem=z_r.at[z],
                device_id=(row_of(y, z + k), col), device_id_type=MESH)

        order = sorted(range(1, NZ), key=lambda k: -min(k, NZ - k))
        for k in order:
            along(k).start()
        for k in reversed(order):
            src = lax.rem(z + k, NZ)
            pltpu.make_async_remote_copy(
                src_ref=zbuf.at[src], dst_ref=zbuf.at[src], send_sem=z_s.at[k], recv_sem=z_r.at[src],
                device_id=(row_of(y, z + k), col), device_id_type=MESH).wait_recv()
        total = zbuf[0]
        for k in range(1, NZ):
            total = total + zbuf[k]
        gram_ref[mine, :] = total

        def back(dx, dy, c):
            to = x * 2 + other if (dx, dy) == (0, 0) else lax.rem(x + dx, NX) * 2 + c
            return pltpu.make_async_remote_copy(
                src_ref=gram_ref.at[mine, :], dst_ref=gram_ref.at[mine, :], send_sem=ag_s.at[(dx * NY + dy) * 2 + c],
                recv_sem=ag_r.at[dx * NY + dy], device_id=(row_of(y + dy, z), to), device_id_type=MESH)

        backs = [(dx, dy, c) for dx, dy in spots for c in (0, 1) if (dx, dy, c) != (0, 0, 0)]
        for spot in backs:
            back(*spot).start()
        for k in order:
            along(k).wait_send()
        for spot in backs:
            back(*spot).wait_send()

    def arrive(dx, dy):
        lines = tile_of(lax.rem(x - dx + NX, NX), lax.rem(y - dy + NY, NY))
        pltpu.make_async_remote_copy(
            src_ref=gram_ref.at[lines, :], dst_ref=gram_ref.at[lines, :], send_sem=ag_s.at[0],
            recv_sem=ag_r.at[dx * NY + dy], device_id=(row, x * 2 + other), device_id_type=MESH).wait_recv()

    for dx, dy in spots[-2::-1]:
        arrive(dx, dy)

    @pl.when(jnp.logical_not(owner))
    def _():
        arrive(0, 0)
        scatter(0, 0).wait_send()

    for i in range(N_PLAN):
        message(i).wait_send()
    swap.wait_send()
    for send in sends:
        send.wait_send()
    for dx, dy in spots[:-1]:
        scatter(dx, dy).wait_send()


def factor_kernel(nodes, gram_ref, image_ref, basis_ref, factor_ref, inv_ref):
    tiles = BLK // 8
    full = (8, BLK)
    left = [gram_ref[pl.ds(k * 8, 8), :] * (1.0 / nodes) for k in range(tiles)]
    row_ids = lax.broadcasted_iota(jnp.int32, full, 0)
    lane_ids = lax.broadcasted_iota(jnp.int32, full, 1)
    right = [jnp.where(row_ids + 8 * k == lane_ids, 1.0, 0.0) for k in range(tiles)]
    for t in range(tiles):
        base = t * 8
        lrow = [jnp.broadcast_to(left[t][r:r + 1, :], full) for r in range(8)]
        rrow = [jnp.broadcast_to(right[t][r:r + 1, :], full) for r in range(8)]
        entry = {(i, j): jnp.broadcast_to(lrow[i][:, base + j:base + j + 1], full) for i in range(8) for j in range(i, 8)}
        mult = {}
        recip = []
        for j in range(8):
            root = lax.rsqrt(entry[j, j])
            inv = root * root
            recip.append(inv)
            pairs = {(i, k): entry[j, i] * entry[j, k] for i in range(j + 1, 8) for k in range(i, 8)}
            for i, k in pairs:
                entry[i, k] = entry[i, k] - pairs[i, k] * inv
            for i in range(j + 1, 8):
                mult[i, j] = entry[j, i] * inv
                lrow[i] = lrow[i] - mult[i, j] * lrow[j]
                rrow[i] = rrow[i] - mult[i, j] * rrow[j]
            factor_ref[pl.ds(base + j, 1), :] = jnp.where(lane_ids[:1] >= base + j, (lrow[j] * root)[:1], 0.0)
            inv_ref[pl.ds(base + j, 1), :] = (rrow[j] * root)[:1]
        if t == tiles - 1:
            break
        for j in range(7, -1, -1):
            lrow[j] = lrow[j] * recip[j]
            rrow[j] = rrow[j] * recip[j]
            for i in range(7, j, -1):
                lrow[j] = lrow[j] - mult[i, j] * lrow[i]
                rrow[j] = rrow[j] - mult[i, j] * rrow[i]
        for k in range(t + 1, tiles):
            old = left[k]
            for j in range(7, -1, -1):
                by = jnp.broadcast_to(old[:, base + j:base + j + 1], full)
                left[k] = left[k] - by * lrow[j]
                right[k] = right[k] - by * rrow[j]
    basis_ref[...] = lax.dot_general(image_ref[...], inv_ref[...], (((1,), (1,)), ((), ())), precision=HIGHEST,
                                     preferred_element_type=jnp.float32)


def local(sketch, degree, block_vals, block_rows, block_cols, live_count):
    f32 = jnp.float32
    square = jax.ShapeDtypeStruct((BLK, BLK), f32)
    vmem = pl.BlockSpec(memory_space=pltpu.VMEM)
    dma = pltpu.SemaphoreType.DMA
    gram, image = pl.pallas_call(
        comm_kernel,
        out_shape=(pltpu.VMEM((BLK, BLK), f32), pltpu.VMEM((BLK, BLK), f32)),
        in_specs=[pl.BlockSpec(memory_space=pl.ANY)] * 6,
        out_specs=(vmem, vmem),
        scratch_shapes=[
            pltpu.VMEM((BLK, BLK), jnp.bfloat16),
            pltpu.VMEM((1, BLK), f32),
            pltpu.SMEM((1, 1, SLOTS), jnp.int32),
            pltpu.SMEM((1, 1, SLOTS), jnp.int32),
            pltpu.SMEM((1, 1), jnp.int32),
            pltpu.VMEM((NY, NZ, BLK, BLK), jnp.bfloat16),
            pltpu.VMEM((SLOTS, BLK, BLK), jnp.bfloat16),
            pltpu.VMEM((SLOTS, BLK, BLK), f32),
            pltpu.VMEM((2, NX, BLK, BLK), f32),
            pltpu.VMEM((NX, BLK, BLK), f32),
            pltpu.VMEM((NX, BLK, BLK), f32),
            pltpu.VMEM((NX, BLK, BLK), f32),
            pltpu.VMEM((BLK, BLK), f32),
            pltpu.VMEM((2 * NX * NY, 8, BLK), f32),
            pltpu.VMEM((NZ, 8, BLK), f32),
            dma((6,)), dma((N_PLAN,)), dma((N_PLAN,)), dma, dma, dma((NX,)), dma((NX,)),
            dma((NX * NY,)), dma((2 * NX * NY,)), dma((NZ,)), dma((NZ,)), dma((2 * NX * NY,)), dma((NX * NY,)),
        ],
        compiler_params=pltpu.CompilerParams(collective_id=0, has_side_effects=True),
        name="spread",
    )(sketch, degree.reshape(1, BLK), block_vals.reshape(SLOTS, BLK, BLK), block_rows, block_cols,
      live_count)
    gram = pltpu.with_memory_space_constraint(gram, pltpu.VMEM)
    image = pltpu.with_memory_space_constraint(image, pltpu.VMEM)
    nodes = BLK * lax.axis_size("row") * lax.axis_size("col")
    return pl.pallas_call(
        functools.partial(factor_kernel, nodes),
        out_shape=(square, square),
        in_specs=[vmem, vmem],
        out_specs=(vmem, vmem),
        scratch_shapes=[pltpu.VMEM((BLK, BLK), f32)],
        name="orthonormalize",
    )(gram, image)


def solution(mesh):
    in_specs = (
        P(("row", "col"), None),
        P(("row", "col")),
        P("row", "col", None, None, None),
        P("row", "col", None),
        P("row", "col", None),
        P("row", "col"),
    )
    out_specs = (P(("row", "col"), None), P())
    return jax.shard_map(local, mesh=mesh, in_specs=in_specs, out_specs=out_specs, check_vma=False)
```

```python
import functools

import jax
import jax.numpy as jnp
from jax import lax
from jax.experimental import pallas as pl
from jax.experimental.pallas import tpu as pltpu
from jax.sharding import PartitionSpec as P

MESH = pl.DeviceIdType.MESH
HIGHEST = lax.Precision.HIGHEST
NX, NY, NZ = 4, 4, 16
BLK = 128
SLOTS = 16

PLAN = (
    (2, 0, 0, 0, 1, 96, 112),
    (-2, 0, 0, 0, 1, 112, 128),
    (0, 3, 0, 0, 1, 0, 96),
    (0, -3, 0, 0, 1, 0, 96),
    (1, 0, 0, 0, 1, 96, 128),
    (-1, 0, 0, 0, 1, 96, 128),
    (0, 2, 0, 0, 1, 0, 96),
    (0, -2, 0, 0, 1, 0, 96),
    (0, 1, 0, 0, 1, 0, 96),
    (0, -1, 0, 0, 1, 0, 96),
    (2, 0, 0, 0, 1, 0, 48),
    (-2, 0, 0, 0, 1, 48, 96),
    (1, 0, 0, 0, 1, 0, 96),
    (-1, 0, 0, 0, 1, 0, 96),
    (0, 1, None, 0, 1, 96, 128),
    (0, -1, None, 0, 1, 96, 128),
    (0, 1, 0, -3, 1, 0, 96),
    (0, -1, 0, 3, 1, 0, 96),
    (0, 3, 0, -3, 1, 0, 96),
    (0, -3, 0, 3, 1, 0, 96),
    (1, 0, 0, 3, 1, 0, 96),
    (-1, 0, 0, 3, 1, 0, 96),
    (1, 0, 0, -3, 1, 0, 96),
    (-1, 0, 0, -3, 1, 0, 96),
    (1, 0, 0, -2, 2, 0, 96),
    (1, 0, 0, 1, 2, 0, 96),
    (-1, 0, 0, 1, 2, 0, 96),
    (0, 2, None, -1, 1, 96, 128),
    (0, -2, None, 1, 1, 96, 128),
    (-1, 0, 0, -2, 2, 0, 96),
    (0, 1, 0, -4, 1, 0, 96),
    (0, -1, 0, 4, 1, 0, 96),
    (0, 3, 0, -4, 1, 0, 96),
    (0, -3, 0, 4, 1, 0, 96),
    (2, 0, 0, 4, 1, 0, 48),
    (-2, 0, 0, 4, 1, 48, 96),
    (2, 0, 0, -4, 1, 0, 48),
    (-2, 0, 0, -4, 1, 48, 96),
    (1, 0, 0, 4, 1, 0, 96),
    (-1, 0, 0, 4, 1, 0, 96),
    (1, 0, 0, -4, 1, 0, 96),
    (-1, 0, 0, -4, 1, 0, 96),
    (1, 0, -1, -2, 2, 0, 48),
    (-1, 0, 1, 1, 2, 48, 96),
    (1, 0, -1, 3, 1, 0, 48),
    (-1, 0, 1, 3, 1, 48, 96),
    (0, 2, None, -3, 1, 96, 128),
    (0, -2, None, 3, 1, 96, 128),
    (0, -1, None, -3, 1, 96, 128),
    (0, 3, 0, -5, 1, 0, 48),
    (0, -3, 0, 5, 1, 48, 96),
    (1, 0, 0, 5, 2, 0, 96),
    (-1, 0, 0, 5, 2, 0, 96),
    (1, 0, 0, -6, 2, 0, 96),
    (-1, 0, 0, -6, 2, 0, 96),
    (0, 1, None, 3, 1, 96, 128),
    (0, 1, None, -3, 1, 96, 128),
    (1, 0, 0, -7, 1, 0, 96),
    (1, 0, 0, 7, 1, 0, 96),
    (-1, 0, 0, 7, 1, 0, 96),
    (-1, 0, 0, -7, 1, 0, 96),
    (0, -1, None, 3, 1, 96, 128),
    (1, 0, -1, 1, 2, 0, 48),
    (-1, 0, 1, -2, 2, 48, 96),
    (0, 3, None, -5, 1, 96, 112),
    (0, -3, None, 5, 1, 112, 128),
    (0, 2, None, -5, 1, 96, 128),
    (0, -2, None, 5, 1, 96, 128),
    (0, 1, None, -5, 1, 96, 128),
    (0, -1, None, 5, 1, 96, 128),
    (1, 0, -1, 5, 2, 0, 48),
    (-1, 0, 1, 5, 2, 48, 96),
    (2, 0, 0, 8, 1, 0, 48),
    (1, 0, -1, -3, 1, 0, 48),
    (1, 0, -1, -6, 2, 0, 48),
    (-1, 0, 1, -6, 2, 48, 96),
    (-1, 0, 1, -3, 1, 48, 96),
    (-2, 0, 0, 8, 1, 48, 96),
    (1, 0, 0, 8, 1, 0, 96),
    (-1, 0, 0, 8, 1, 0, 96),
    (1, 0, -1, 7, 1, 0, 48),
    (-1, 0, 1, 7, 1, 48, 96),
    (1, 0, -1, -7, 1, 0, 48),
    (-1, 0, 1, -7, 1, 48, 96),
)
N_PLAN = len(PLAN)
LOW = NZ // 2 - 1


def wrap(value, n):
    value = value % n
    return value - n if value > n // 2 else value


def row_of(y, z):
    return lax.rem(y + 4 * NY, NY) * NZ + lax.rem(z + 4 * NZ, NZ)


def comm_kernel(sk_any, deg_any, vals_any, rows_any, cols_any, live_any, gram_ref, image_ref,
                sk_ref, deg_ref, rows_ref, cols_ref, live_ref, gat, vals, prods, part, crecv, comb, xrecv, glocal, rsbuf, zbuf,
                vsem, gs, gr, cs, cr, xs, xr, rs_s, rs_r, z_s, z_r, ag_s, ag_r):
    row = lax.axis_index("row")
    col = lax.axis_index("col")
    y, z = row // NZ, lax.rem(row, NZ)
    x, core = col // 2, lax.rem(col, 2)

    loads = [pltpu.make_async_copy(src, dst, vsem.at[i]) for i, (src, dst) in enumerate((
        (deg_any, deg_ref), (sk_any, sk_ref), (vals_any, vals), (rows_any, rows_ref), (cols_any, cols_ref),
        (live_any, live_ref)))]
    for load in loads:
        load.start()
    barrier = pltpu.get_barrier_semaphore()
    moves = sorted({(wrap(d * m[0], NY), wrap(d * m[1], NZ)) for m in PLAN for d in (1, -1)})
    peers = [(row_of(y + dy, z + dz), col) for dy, dz in moves]
    peers += [(row, lax.rem(col + k, 2 * NX)) for k in range(1, 2 * NX)]
    for peer in peers:
        pl.semaphore_signal(barrier, inc=1, device_id=peer, device_id_type=MESH)
    loads[0].wait()
    loads[1].wait()
    ids_r = lax.broadcasted_iota(jnp.int32, (BLK, BLK), 0)
    ids_c = lax.broadcasted_iota(jnp.int32, (BLK, BLK), 1)
    spread = jnp.where(ids_r == ids_c, jnp.broadcast_to(deg_ref[...], (BLK, BLK)), 0.0)
    scale = lax.rsqrt(jnp.sum(spread, axis=1, keepdims=True))
    gat[y, LOW] = (scale * sk_ref[...].astype(jnp.float32)).astype(jnp.bfloat16)
    pl.semaphore_wait(barrier, len(peers))

    def blocks(oy, oz, count, lo, hi):
        ys = slice(None) if oy is None else lax.rem(y + oy + NY, NY)
        return gat.at[ys, pl.ds(oz + LOW, count), pl.ds(lo, hi - lo), :]

    def message(i):
        dy, dz, oy, oz, count, lo, hi = PLAN[i]
        return pltpu.make_async_remote_copy(
            src_ref=blocks(oy, oz, count, lo, hi), dst_ref=blocks(oy, wrap(oz - dz, NZ), count, lo, hi),
            send_sem=gs.at[i], recv_sem=gr.at[i],
            device_id=(row_of(y + dy, z + dz), col), device_id_type=MESH)

    def landed(i):
        dy, dz, oy, oz, count, lo, hi = PLAN[i]
        block = blocks(None if oy is None else oy - dy, wrap(oz - dz, NZ), count, lo, hi)
        pltpu.make_async_remote_copy(
            src_ref=block, dst_ref=block, send_sem=gs.at[i], recv_sem=gr.at[i],
            device_id=(row_of(y + dy, z + dz), col), device_id_type=MESH).wait_recv()

    def places(oy, oz, count):
        return {(wrap(v, NY), wrap(oz + k, NZ)) for v in (range(NY) if oy is None else (oy,)) for k in range(count)}

    waited = set()
    for i, (_, _, oy, oz, count, lo, hi) in enumerate(PLAN):
        for j, (dy, dz, py, pz, many, plo, phi) in enumerate(PLAN):
            brought = places(None if py is None else py - dy, pz - dz, many)
            if j not in waited and plo < hi and lo < phi and brought & places(oy, oz, count):
                landed(j)
                waited.add(j)
        message(i).start()
    for j in range(N_PLAN):
        if j not in waited:
            landed(j)

    for load in loads[2:]:
        load.wait()
    for s in range(SLOTS):
        at = cols_ref[0, 0, s]
        picked = gat[at // NZ, lax.rem(lax.rem(at, NZ) - z + LOW + NZ, NZ)]
        prods[s] = jnp.dot(vals[s], picked, preferred_element_type=jnp.float32)
    live = live_ref[0, 0]
    for r in range(2 * NX):
        weights = [jnp.where((rows_ref[0, 0, s] == r) & (s < live), 1.0, 0.0) for s in range(SLOTS)]
        for k in range(BLK // 16):
            lines = pl.ds(k * 16, 16)
            total = weights[0] * prods[0, lines, :]
            for s in range(1, SLOTS):
                total = total + weights[s] * prods[s, lines, :]
            part[r % 2, r // 2, lines, :] = total

    other = 1 - core
    swap = pltpu.make_async_remote_copy(
        src_ref=part.at[other], dst_ref=crecv, send_sem=cs, recv_sem=cr,
        device_id=(row, x * 2 + other), device_id_type=MESH)
    swap.start()
    swap.wait_recv()
    sends = []
    for k in (2, 1, 3):
        to = lax.rem(x + k, NX)
        comb[k] = part[core, to] + crecv[to]
        send = pltpu.make_async_remote_copy(
            src_ref=comb.at[k], dst_ref=xrecv.at[k], send_sem=xs.at[k], recv_sem=xr.at[k],
            device_id=(row, to * 2 + core), device_id_type=MESH)
        send.start()
        sends.append(send)
    total = part[core, x] + crecv[x]
    for send in (sends[1], sends[2], sends[0]):
        send.wait_recv()
    for k in (1, 2, 3):
        total = total + xrecv[k]
    image = scale * total
    image_ref[...] = image
    glocal[...] = lax.dot_general(image, image, (((0,), (0,)), ((), ())), precision=HIGHEST,
                                  preferred_element_type=jnp.float32)

    chip = x * NY + y
    owner = core == lax.rem(x + y, 2)
    spots = sorted(((dx, dy) for dx in range(NX) for dy in range(NY)),
                   key=lambda d: -min(d[0], NX - d[0]) - min(d[1], NY - d[1]))

    def tile_of(tx, ty):
        return pl.ds(pl.multiple_of((tx * NY + ty) * 8, 8), 8)

    def scatter(dx, dy):
        tx, ty = lax.rem(x + dx, NX), lax.rem(y + dy, NY)
        slot = (dx * NY + dy) * 2 + core
        return pltpu.make_async_remote_copy(
            src_ref=glocal.at[tile_of(tx, ty), :], dst_ref=rsbuf.at[slot],
            send_sem=rs_s.at[dx * NY + dy], recv_sem=rs_r.at[slot],
            device_id=(row_of(ty, z), tx * 2 + lax.rem(tx + ty, 2)), device_id_type=MESH)

    for dx, dy in spots[:-1]:
        scatter(dx, dy).start()

    @pl.when(jnp.logical_not(owner))
    def _():
        scatter(0, 0).start()

    mine = tile_of(x, y)

    def collect(slot):
        pltpu.make_async_remote_copy(
            src_ref=rsbuf.at[slot], dst_ref=rsbuf.at[slot], send_sem=rs_s.at[0], recv_sem=rs_r.at[slot],
            device_id=(row, x * 2 + other), device_id_type=MESH).wait_recv()

    @pl.when(owner)
    def _():
        collect(other)
        total = glocal[mine, :] + rsbuf[other]
        for dx, dy in spots[-2::-1]:
            for c in (0, 1):
                collect((dx * NY + dy) * 2 + c)
                total = total + rsbuf[(dx * NY + dy) * 2 + c]
        zbuf[z] = total

        def along(k):
            return pltpu.make_async_remote_copy(
                src_ref=zbuf.at[z], dst_ref=zbuf.at[z], send_sem=z_s.at[k], recv_sem=z_r.at[z],
                device_id=(row_of(y, z + k), col), device_id_type=MESH)

        order = sorted(range(1, NZ), key=lambda k: -min(k, NZ - k))
        for k in order:
            along(k).start()
        for k in reversed(order):
            src = lax.rem(z + k, NZ)
            pltpu.make_async_remote_copy(
                src_ref=zbuf.at[src], dst_ref=zbuf.at[src], send_sem=z_s.at[k], recv_sem=z_r.at[src],
                device_id=(row_of(y, z + k), col), device_id_type=MESH).wait_recv()
        total = zbuf[0]
        for k in range(1, NZ):
            total = total + zbuf[k]
        gram_ref[mine, :] = total

        def back(dx, dy, c):
            to = x * 2 + other if (dx, dy) == (0, 0) else lax.rem(x + dx, NX) * 2 + c
            return pltpu.make_async_remote_copy(
                src_ref=gram_ref.at[mine, :], dst_ref=gram_ref.at[mine, :], send_sem=ag_s.at[(dx * NY + dy) * 2 + c],
                recv_sem=ag_r.at[dx * NY + dy], device_id=(row_of(y + dy, z), to), device_id_type=MESH)

        backs = [(dx, dy, c) for dx, dy in spots for c in (0, 1) if (dx, dy, c) != (0, 0, 0)]
        for spot in backs:
            back(*spot).start()
        for k in order:
            along(k).wait_send()
        for spot in backs:
            back(*spot).wait_send()

    def arrive(dx, dy):
        lines = tile_of(lax.rem(x - dx + NX, NX), lax.rem(y - dy + NY, NY))
        pltpu.make_async_remote_copy(
            src_ref=gram_ref.at[lines, :], dst_ref=gram_ref.at[lines, :], send_sem=ag_s.at[0],
            recv_sem=ag_r.at[dx * NY + dy], device_id=(row, x * 2 + other), device_id_type=MESH).wait_recv()

    for dx, dy in spots[-2::-1]:
        arrive(dx, dy)

    @pl.when(jnp.logical_not(owner))
    def _():
        arrive(0, 0)
        scatter(0, 0).wait_send()

    for i in range(N_PLAN):
        message(i).wait_send()
    swap.wait_send()
    for send in sends:
        send.wait_send()
    for dx, dy in spots[:-1]:
        scatter(dx, dy).wait_send()


def factor_kernel(nodes, gram_ref, image_ref, basis_ref, factor_ref, inv_ref):
    tiles = BLK // 8
    full = (8, BLK)
    left = [gram_ref[pl.ds(k * 8, 8), :] * (1.0 / nodes) for k in range(tiles)]
    row_ids = lax.broadcasted_iota(jnp.int32, full, 0)
    lane_ids = lax.broadcasted_iota(jnp.int32, full, 1)
    right = [jnp.where(row_ids + 8 * k == lane_ids, 1.0, 0.0) for k in range(tiles)]
    for t in range(tiles):
        base = t * 8
        lrow = [jnp.broadcast_to(left[t][r:r + 1, :], full) for r in range(8)]
        rrow = [jnp.broadcast_to(right[t][r:r + 1, :], full) for r in range(8)]
        entry = {(i, j): jnp.broadcast_to(lrow[i][:, base + j:base + j + 1], full) for i in range(8) for j in range(i, 8)}
        mult = {}
        recip = []
        for j in range(8):
            root = lax.rsqrt(entry[j, j])
            inv = root * root
            recip.append(inv)
            pairs = {(i, k): entry[j, i] * entry[j, k] for i in range(j + 1, 8) for k in range(i, 8)}
            for i, k in pairs:
                entry[i, k] = entry[i, k] - pairs[i, k] * inv
            for i in range(j + 1, 8):
                mult[i, j] = entry[j, i] * inv
                lrow[i] = lrow[i] - mult[i, j] * lrow[j]
                rrow[i] = rrow[i] - mult[i, j] * rrow[j]
            factor_ref[pl.ds(base + j, 1), :] = jnp.where(lane_ids[:1] >= base + j, (lrow[j] * root)[:1], 0.0)
            inv_ref[pl.ds(base + j, 1), :] = (rrow[j] * root)[:1]
        if t == tiles - 1:
            break
        for j in range(7, -1, -1):
            lrow[j] = lrow[j] * recip[j]
            rrow[j] = rrow[j] * recip[j]
            for i in range(7, j, -1):
                lrow[j] = lrow[j] - mult[i, j] * lrow[i]
                rrow[j] = rrow[j] - mult[i, j] * rrow[i]
        for k in range(t + 1, tiles):
            old = left[k]
            for j in range(7, -1, -1):
                by = jnp.broadcast_to(old[:, base + j:base + j + 1], full)
                left[k] = left[k] - by * lrow[j]
                right[k] = right[k] - by * rrow[j]
    basis_ref[...] = lax.dot_general(image_ref[...], inv_ref[...], (((1,), (1,)), ((), ())), precision=HIGHEST,
                                     preferred_element_type=jnp.float32)


def local(sketch, degree, block_vals, block_rows, block_cols, live_count):
    f32 = jnp.float32
    square = jax.ShapeDtypeStruct((BLK, BLK), f32)
    vmem = pl.BlockSpec(memory_space=pltpu.VMEM)
    dma = pltpu.SemaphoreType.DMA
    gram, image = pl.pallas_call(
        comm_kernel,
        out_shape=(pltpu.VMEM((BLK, BLK), f32), pltpu.VMEM((BLK, BLK), f32)),
        in_specs=[pl.BlockSpec(memory_space=pl.ANY)] * 6,
        out_specs=(vmem, vmem),
        scratch_shapes=[
            pltpu.VMEM((BLK, BLK), jnp.bfloat16),
            pltpu.VMEM((1, BLK), f32),
            pltpu.SMEM((1, 1, SLOTS), jnp.int32),
            pltpu.SMEM((1, 1, SLOTS), jnp.int32),
            pltpu.SMEM((1, 1), jnp.int32),
            pltpu.VMEM((NY, NZ, BLK, BLK), jnp.bfloat16),
            pltpu.VMEM((SLOTS, BLK, BLK), jnp.bfloat16),
            pltpu.VMEM((SLOTS, BLK, BLK), f32),
            pltpu.VMEM((2, NX, BLK, BLK), f32),
            pltpu.VMEM((NX, BLK, BLK), f32),
            pltpu.VMEM((NX, BLK, BLK), f32),
            pltpu.VMEM((NX, BLK, BLK), f32),
            pltpu.VMEM((BLK, BLK), f32),
            pltpu.VMEM((2 * NX * NY, 8, BLK), f32),
            pltpu.VMEM((NZ, 8, BLK), f32),
            dma((6,)), dma((N_PLAN,)), dma((N_PLAN,)), dma, dma, dma((NX,)), dma((NX,)),
            dma((NX * NY,)), dma((2 * NX * NY,)), dma((NZ,)), dma((NZ,)), dma((2 * NX * NY,)), dma((NX * NY,)),
        ],
        compiler_params=pltpu.CompilerParams(collective_id=0, has_side_effects=True),
        name="spread",
    )(sketch, degree.reshape(1, BLK), block_vals.reshape(SLOTS, BLK, BLK), block_rows, block_cols,
      live_count)
    gram = pltpu.with_memory_space_constraint(gram, pltpu.VMEM)
    image = pltpu.with_memory_space_constraint(image, pltpu.VMEM)
    nodes = BLK * lax.axis_size("row") * lax.axis_size("col")
    return pl.pallas_call(
        functools.partial(factor_kernel, nodes),
        out_shape=(square, square),
        in_specs=[vmem, vmem],
        out_specs=(vmem, vmem),
        scratch_shapes=[pltpu.VMEM((BLK, BLK), f32)],
        name="orthonormalize",
    )(gram, image)


def solution(mesh):
    in_specs = (
        P(("row", "col"), None),
        P(("row", "col")),
        P("row", "col", None, None, None),
        P("row", "col", None),
        P("row", "col", None),
        P("row", "col"),
    )
    out_specs = (P(("row", "col"), None), P())
    return jax.shard_map(local, mesh=mesh, in_specs=in_specs, out_specs=out_specs, check_vma=False)
```
